32 devices in a mesh: dp: 16 (over z, x, core), tensor: 2 (over y).
Axes of the slice: x: 2, y: 2, z: 4, core: 2. Of those that a mesh axis runs over, the one named last changes fastest.
Arguments:
- inputs: bfloat16 [730, 32, 1152], P('tensor', 'dp'), may hold values from -6 to 6
- lengths: int32 [32], P('dp'), may hold values from 364 to 729, as said below
- cotangent: bfloat16 [730, 32, 1152], P('tensor', 'dp'), may hold values from -6 to 6
- ln_gain: float32 [2, 1152], replicated, may hold values from 0.1 to 1.9
- ln_bias: float32 [2, 1152], replicated, may hold values from -3 to 3
- w_qkv: bfloat16 [1152, 3, 1152], P('dp', None, 'tensor')
- qv_bias: float32 [2, 1152], P(None, 'tensor'), may hold values from -2 to 2
- w_out: bfloat16 [1152, 1152], P('tensor', 'dp'), may hold values from -0.75 to 0.75
- out_bias: float32 [2, 1152], replicated, may hold values from -3 to 3
- w_up: bfloat16 [1152, 4304], P('dp', 'tensor'), may hold values from -0.1875 to 0.1875
- up_bias: float32 [4304], P('tensor'), may hold values from -3 to 3
- w_down: bfloat16 [4304, 1152], P('tensor', 'dp'), may hold values from -0.09375 to 0.09375
Outputs:
- output: bfloat16 [730, 32, 1152], P('tensor', 'dp')
- d_inputs: bfloat16 [730, 32, 1152], P('tensor', 'dp')
- g_ln_gain: float32 [2, 1152], replicated
- g_ln_bias: float32 [2, 1152], replicated
- g_qkv: float32 [1152, 3, 1152], P('dp', None, 'tensor')
- g_qv_bias: float32 [2, 1152], P(None, 'tensor')
- g_out: float32 [1152, 1152], P('tensor', 'dp')
- g_out_bias: float32 [2, 1152], replicated
- g_up: float32 [1152, 4304], P('dp', 'tensor')
- g_up_bias: float32 [4304], P('tensor')
- g_down: float32 [4304, 1152], P('tensor', 'dp')
The draws below stay inside these ranges and needn't reach their ends.
Inputs may be any that keep to these rules, and one draw needn't show every extreme that they name: Each image's valid tokens are its positions 0 to lengths - 1; some image has exactly 729.
All inputs are finite; a program needn't handle non-finite values.
Results may differ from the reference program's by a relative error of at most 0.015.
Values may be sent and summed in bfloat16 or wider, within the bound.
No kernel may reach another device: no remote copies, remote signals or barrier semaphores. Data moves between devices by JAX's collectives and lax.ppermute only.
A program may use at most 256 MiB of HBM per device.

```python
import jax
import jax.numpy as jnp
from jax import lax

D = 1152
HEADS = 16
HD = 72
FF = 4304
LEN = 729
IMAGES = 32
SEQ = 730


def draw_w_qkv(key, part):
    base = jax.random.normal(key, (D, 3, D), jnp.float32) * D ** (-0.5)
    return base.astype(jnp.bfloat16)


def draw_lengths(key, part):
    drawn = jax.random.randint(key, (IMAGES,), LEN // 2, LEN + 1, dtype=jnp.int32)
    return drawn.at[0].set(LEN)


def levels(own_key, dims, cuts, least, high):
    level, own = 1.0, jax.random.fold_in(own_key, 6)
    for dim, parts in cuts:
        steps = jnp.exp(jax.random.uniform(jax.random.fold_in(own, dim), (parts,), jnp.float32, least / len(cuts), high / len(cuts)))
        level = level * jnp.repeat(steps, dims[dim] // parts).reshape([-1 if axis == dim else 1 for axis in range(len(dims))])
    return level


def scatter_about(key, shape, scale, limit, pieces=(), kind=jnp.bfloat16):
    array = jax.random.normal(key, shape, jnp.float32) * scale
    if len(pieces) > 0:
        array = levels(key, shape, pieces, -0.22, 0.18) * array
    return jnp.clip(array, min=-limit, max=limit).astype(kind)


def setup_inputs(seed: int = 0) -> dict:
    streams_of = jax.random.split(jax.random.key(seed), 13)
    return {
        "inputs": scatter_about(streams_of[0], (SEQ, IMAGES, D), 1.0, 6.0, ((0, 2), (1, 16))),
        "lengths": draw_lengths(jax.random.fold_in(streams_of[12], 71), 0),
        "cotangent": scatter_about(streams_of[2], (SEQ, IMAGES, D), 1.0, 6.0, ((0, 2), (1, 16))),
        "ln_gain": jnp.clip(1.0 + 0.18 * jax.random.normal(streams_of[3], (2, D), jnp.float32), 0.1, 1.9),
        "ln_bias": scatter_about(streams_of[4], (2, D), 0.3, 3.0, (), jnp.float32),
        "w_qkv": draw_w_qkv(jax.random.fold_in(streams_of[12], 71), 0),
        "qv_bias": scatter_about(streams_of[6], (2, D), 0.2, 2.0, ((1, 2),), jnp.float32),
        "w_out": scatter_about(streams_of[7], (D, D), (D // 16) ** -0.5, 0.75, ((0, 2), (1, 16))),
        "out_bias": scatter_about(streams_of[8], (2, D), 0.3, 3.0, (), jnp.float32),
        "w_up": scatter_about(streams_of[9], (D, FF), D ** -0.5, 0.1875, ((0, 16), (1, 2))),
        "up_bias": scatter_about(streams_of[10], (FF,), 0.5, 3.0, ((0, 2),), jnp.float32),
        "w_down": scatter_about(streams_of[11], (FF, D), FF ** -0.5, 0.09375, ((0, 2), (1, 16))),
    }


epsilon = 1e-06

def normalize(values, gain, shift):
    mean = lax.optimization_barrier(jnp.mean(values, axis=-1, keepdims=True))
    centred = values - mean
    variance = lax.optimization_barrier(jnp.mean(centred * centred, axis=-1, keepdims=True))
    return centred * lax.rsqrt(variance + epsilon) * gain + shift

def gelu_tanh(values):
    return jax.nn.gelu(values, approximate=True)

def rounded(values):
    return lax.optimization_barrier(values.astype(jnp.bfloat16)).astype(jnp.float32)

def reference(inputs, lengths, cotangent, ln_gain, ln_bias, w_qkv, qv_bias, w_out, out_bias, w_up, up_bias, w_down):
    fl = jnp.float32
    scale = HD ** (-0.5)
    weight_qkv = w_qkv.astype(fl)
    weight_out = w_out.astype(fl)
    weight_up = w_up.astype(fl)
    weight_down = w_down.astype(fl)
    bias_three = jnp.stack([qv_bias[0], jnp.zeros((D,), fl), qv_bias[1]])
    position = jnp.arange(SEQ, dtype=jnp.int32)

    def one_image(carry, item):
        image, length, cot = item
        valid = position < length
        row_valid = valid.astype(fl)[:, None]
        x_float = image.astype(fl)
        xn1 = rounded(normalize(x_float, ln_gain[0], ln_bias[0]))
        qkv = rounded(jnp.einsum('sd,dkc->skc', xn1, weight_qkv) + bias_three)
        query = qkv[:, 0].reshape(SEQ, HEADS, HD)
        keys = qkv[:, 1].reshape(SEQ, HEADS, HD)
        values = qkv[:, 2].reshape(SEQ, HEADS, HD)
        raw = jnp.einsum('qhe,khe->hqk', query, keys) * scale
        raw = jnp.where(valid[None, None, :], raw, -jnp.inf)
        top = lax.optimization_barrier(jnp.max(raw, axis=-1, keepdims=True))
        lse = top + jnp.log(lax.optimization_barrier(jnp.sum(jnp.exp(raw - top), axis=-1, keepdims=True)))
        probs_f = jnp.exp(raw - lse)
        probs = rounded(probs_f)
        attended = rounded(jnp.einsum('hqk,khe->qhe', probs, values)).reshape(SEQ, D)
        h1 = x_float + jnp.dot(attended, weight_out) + out_bias[0]
        xn2 = rounded(normalize(h1, ln_gain[1], ln_bias[1]))
        pre = jnp.dot(xn2, weight_up) + up_bias
        act = rounded(gelu_tanh(pre))
        y_float = h1 + jnp.dot(act, weight_down) + out_bias[1]
        output = (y_float * row_valid).astype(jnp.bfloat16)
        dy = cot.astype(fl) * row_valid
        grad_down = jnp.dot(act.T, dy)
        d_act = jnp.dot(dy, weight_down.T)
        d_pre = jax.vjp(gelu_tanh, pre)[1](d_act)[0]
        grad_b1 = lax.optimization_barrier(jnp.sum(d_pre, axis=0))
        d_pre_b = rounded(d_pre)
        grad_up = jnp.dot(xn2.T, d_pre_b)
        d_xn2 = jnp.dot(d_pre_b, weight_up.T)
        d_h1_ln, grad_g2, grad_c2 = jax.vjp(normalize, h1, ln_gain[1], ln_bias[1])[1](d_xn2)
        d_h1 = dy + d_h1_ln
        grad_bo = lax.optimization_barrier(jnp.sum(d_h1, axis=0))
        grad_b2 = lax.optimization_barrier(jnp.sum(dy, axis=0))
        d_h1_b = rounded(d_h1)
        grad_out = jnp.dot(attended.T, d_h1_b)
        d_att = rounded(jnp.dot(d_h1_b, weight_out.T)).reshape(SEQ, HEADS, HD)
        d_probs = jnp.einsum('qhe,khe->hqk', d_att, values)
        delta = lax.optimization_barrier(jnp.sum(probs_f * d_probs, axis=-1, keepdims=True))
        d_raw = rounded(probs_f * (d_probs - delta) * scale)
        d_query = jnp.einsum('hqk,khe->qhe', d_raw, keys)
        d_keys = jnp.einsum('hqk,qhe->khe', d_raw, query)
        d_values = jnp.einsum('hqk,qhe->khe', probs, d_att)
        d_qkv = jnp.stack([d_query, d_keys, d_values], axis=1).reshape(SEQ, 3, D)
        grad_qv = jnp.stack([lax.optimization_barrier(jnp.sum(d_qkv[:, 0], axis=0)), lax.optimization_barrier(jnp.sum(d_qkv[:, 2], axis=0))])
        d_qkv_b = rounded(d_qkv)
        grad_qkv = jnp.einsum('sd,skc->dkc', xn1, d_qkv_b)
        d_xn1 = jnp.einsum('skc,dkc->sd', d_qkv_b, weight_qkv)
        d_x_ln, grad_g1, grad_c1 = jax.vjp(normalize, x_float, ln_gain[0], ln_bias[0])[1](d_xn1)
        d_input = (d_h1 + d_x_ln).astype(jnp.bfloat16)
        small = jnp.stack([grad_g1, grad_g2, grad_c1, grad_c2, grad_bo, grad_b2])
        update = (small, grad_qkv, grad_qv, grad_out, grad_up, grad_b1, grad_down)
        carry = tuple((a + b for a, b in zip(carry, update)))
        return (carry, (output, d_input))
    start = (jnp.zeros((6, D), fl), jnp.zeros((D, 3, D), fl), jnp.zeros((2, D), fl), jnp.zeros((D, D), fl), jnp.zeros((D, FF), fl), jnp.zeros((FF,), fl), jnp.zeros((FF, D), fl))
    items = (jnp.moveaxis(inputs, 1, 0), lengths, jnp.moveaxis(cotangent, 1, 0))
    totals, (outputs, d_inputs) = lax.scan(one_image, start, items)
    small, g_qkv, g_qv, g_out, g_up, g_b1, g_down = totals
    output = jnp.moveaxis(outputs, 0, 1)
    d_in = jnp.moveaxis(d_inputs, 0, 1)
    return (output, d_in, small[0:2], small[2:4], g_qkv, g_qv, g_out, small[4:6], g_up, g_b1, g_down)
```

```python
import functools

import jax
import jax.numpy as jnp
from jax import lax
from jax.experimental import pallas as pl
from jax.experimental.pallas import tpu as pltpu
from jax.sharding import PartitionSpec as P

HD = 72
epsilon = 1e-06
fl = jnp.float32
bf = jnp.bfloat16


def up_to(n, m):
    return -(-n // m) * m


def dot(a, b, ca, cb):
    return lax.dot_general(a, b, (((ca,), (cb,)), ((), ())), preferred_element_type=fl)


def normalize(values, gain, shift):
    mean = jnp.mean(values, axis=-1, keepdims=True)
    centred = values - mean
    variance = jnp.mean(centred * centred, axis=-1, keepdims=True)
    return centred * lax.rsqrt(variance + epsilon) * gain + shift


def normalize_back(values, gain, grad):
    mean = jnp.mean(values, axis=-1, keepdims=True)
    centred = values - mean
    variance = jnp.mean(centred * centred, axis=-1, keepdims=True)
    inverse = lax.rsqrt(variance + epsilon)
    hat = centred * inverse
    scaled = grad * gain
    first = jnp.mean(scaled, axis=-1, keepdims=True)
    second = jnp.mean(scaled * hat, axis=-1, keepdims=True)
    return inverse * (scaled - first - hat * second), hat


def gelu_tanh(values):
    return jax.nn.gelu(values, approximate=True)


def window(head, colp, win):
    start = jnp.minimum(head * HD // 128 * 128, colp - win)
    return pl.multiple_of(start, 128), head * HD - start


def forward_kernel(bias_ref, qkv_ref, out_ref, lse_ref, *, heads, colp, win):
    scale = HD ** (-0.5)
    out_ref[...] = jnp.zeros_like(out_ref)

    def one_head(head, carry):
        at, off = window(head, colp, win)
        lane = lax.broadcasted_iota(jnp.int32, (1, win), 1)
        mine = (lane >= off) & (lane < off + HD)
        query = qkv_ref[:, pl.ds(at, win)]
        keys = qkv_ref[:, pl.ds(pl.multiple_of(colp + at, 128), win)]
        values = qkv_ref[:, pl.ds(pl.multiple_of(2 * colp + at, 128), win)]
        keys = jnp.where(mine, keys, jnp.zeros_like(keys))
        values = jnp.where(mine, values, jnp.zeros_like(values))
        raw = dot(keys, query, 1, 1) * scale + bias_ref[...]
        top = jnp.max(raw, axis=0, keepdims=True)
        weights = jnp.exp(raw - top)
        total = jnp.sum(weights, axis=0, keepdims=True)
        result = dot(values, weights.astype(bf), 0, 0) / total
        lse_ref[pl.ds(head, 1), :] = top + jnp.log(total)
        out_ref[:, pl.ds(at, win)] = out_ref[:, pl.ds(at, win)] + result.T.astype(bf)
        return carry

    lax.fori_loop(0, heads, one_head, 0)


def attention_forward(qkv, bias, image, size, heads):
    colp = qkv.shape[1] // 3
    win = min(256, colp)
    return pl.pallas_call(
        functools.partial(forward_kernel, heads=heads, colp=colp, win=win),
        grid=(1,),
        out_shape=(
            jax.ShapeDtypeStruct((size, colp), bf),
            jax.ShapeDtypeStruct((heads, size), fl),
        ),
        in_specs=[
            pl.BlockSpec((size, 1), lambda g: (image, 0)),
            pl.BlockSpec((size, 3 * colp), lambda g: (image, 0)),
        ],
        out_specs=(
            pl.BlockSpec((size, colp), lambda g: (0, 0)),
            pl.BlockSpec((heads, size), lambda g: (0, 0)),
        ),
        compiler_params=pltpu.CompilerParams(vmem_limit_bytes=56 * 2**20),
        name="attention_forward",
    )(bias, qkv)


def backward_kernel(
    bias_ref, qkv_ref, out_ref, dout_ref, lse_ref, old_ref, dqkv_ref, *, heads, colp, win
):
    scale = HD ** (-0.5)
    dqkv_ref[...] = jnp.zeros_like(dqkv_ref)

    def one_head(head, carry):
        at, off = window(head, colp, win)
        at_k = pl.multiple_of(colp + at, 128)
        at_v = pl.multiple_of(2 * colp + at, 128)
        lane = lax.broadcasted_iota(jnp.int32, (1, win), 1)
        mine = (lane >= off) & (lane < off + HD)

        def keep(block):
            return jnp.where(mine, block, jnp.zeros_like(block))

        query = keep(qkv_ref[:, pl.ds(at, win)])
        keys = keep(qkv_ref[:, pl.ds(at_k, win)])
        values = keep(qkv_ref[:, pl.ds(at_v, win)])
        d_out = keep(dout_ref[:, pl.ds(at, win)])
        product = d_out.astype(fl) * out_ref[:, pl.ds(at, win)].astype(fl)
        delta = jnp.sum(product, axis=1, keepdims=True).T
        raw = dot(keys, query, 1, 1) * scale + bias_ref[...]
        probs = jnp.exp(raw - lse_ref[pl.ds(head, 1), :])
        d_probs = dot(values, d_out, 1, 1)
        d_raw = (probs * ((d_probs - delta) * scale)).astype(bf)

        def add(place, block):
            dqkv_ref[:, pl.ds(place, win)] = dqkv_ref[:, pl.ds(place, win)] + block.astype(bf)

        add(at_v, dot(probs.astype(bf), d_out, 1, 0))
        add(at_k, dot(d_raw, query, 1, 0))
        add(at, dot(keys, d_raw, 0, 0).T)
        return carry

    lax.fori_loop(0, heads, one_head, 0)


def attention_backward(qkv, bias, attended, d_attended, lse, old, image, size, heads):
    colp = qkv.shape[1] // 3
    win = min(256, colp)
    return pl.pallas_call(
        functools.partial(backward_kernel, heads=heads, colp=colp, win=win),
        grid=(1,),
        out_shape=jax.ShapeDtypeStruct(qkv.shape, bf),
        in_specs=[
            pl.BlockSpec((size, 1), lambda g: (image, 0)),
            pl.BlockSpec((size, 3 * colp), lambda g: (image, 0)),
            pl.BlockSpec((size, colp), lambda g: (0, 0)),
            pl.BlockSpec((size, colp), lambda g: (0, 0)),
            pl.BlockSpec((heads, size), lambda g: (0, 0)),
            pl.BlockSpec(memory_space=pl.ANY),
        ],
        out_specs=pl.BlockSpec((size, 3 * colp), lambda g: (image, 0)),
        input_output_aliases={5: 0},
        compiler_params=pltpu.CompilerParams(vmem_limit_bytes=56 * 2**20),
        name="attention_backward",
    )(bias, qkv, attended, d_attended, lse, old)


def from_others(values, parts):
    return [
        lax.ppermute(values, "tensor", [((j + k) % parts, j) for j in range(parts)])
        for k in range(1, parts)
    ]


def all_blocks(values, where, parts):
    images, rows, width = values.shape
    got = [values] + from_others(values, parts)
    full = jnp.zeros((images, rows * parts, width), values.dtype)
    for k, block in enumerate(got):
        start = (where + k) % parts * rows
        full = lax.dynamic_update_slice(full, block, (jnp.int32(0), start, jnp.int32(0)))
    return full


def sum_blocks(values, where, parts, rows):
    def block(k):
        return lax.dynamic_slice_in_dim(values, (where + k) % parts * rows, rows, 1)

    total = block(0)
    for k in range(1, parts):
        pairs = [(j, (j + k) % parts) for j in range(parts)]
        total = total + lax.ppermute(block(k).astype(bf), "tensor", pairs).astype(fl)
    return total


def sum_everywhere(values, axis):
    size = lax.axis_size(axis)
    if size & (size - 1):
        return lax.psum(values, axis)
    step = 1
    while step < size:
        values = values + lax.ppermute(values, axis, [(j, j ^ step) for j in range(size)])
        step *= 2
    return values


def on_device(
    inputs,
    lengths,
    cotangent,
    ln_gain,
    ln_bias,
    w_qkv,
    qv_bias,
    w_out,
    out_bias,
    w_up,
    up_bias,
    w_down,
):
    rows, images, width = inputs.shape
    parts = lax.axis_size("tensor")
    where = lax.axis_index("tensor")
    cols = w_qkv.shape[2]
    hidden = up_bias.shape[0]
    heads = cols // HD
    here = w_qkv.shape[0]
    rowp, colp, hidp = up_to(rows, 16), up_to(cols, 128), up_to(hidden, 128)
    size = rowp * parts
    both = images * size

    def pad_to(values, axis, n):
        widths = [(0, 0)] * values.ndim
        widths[axis] = (0, n - values.shape[axis])
        return jnp.pad(values, widths)

    shard_qkv = pad_to(w_qkv, 2, colp).reshape(here, 3 * colp)
    full_qkv = lax.all_gather(shard_qkv, "dp", axis=0, tiled=True)
    shard_out = pad_to(w_out.T, 1, colp)
    shard_out = jnp.concatenate([shard_out] + from_others(shard_out, parts), axis=1)
    shard_rest = jnp.concatenate(
        [pad_to(w_up, 1, hidp), pad_to(w_down.T, 1, hidp), shard_out], axis=1
    )
    full_rest = lax.all_gather(shard_rest, "dp", axis=0, tiled=True)
    full_up = full_rest[:, :hidp]
    full_down = full_rest[:, hidp : 2 * hidp]
    full_out = full_rest[:, 2 * hidp :]
    own_out = full_rest[:, 2 * hidp : 2 * hidp + colp]

    place = jnp.arange(size, dtype=jnp.int32)
    position = place // rowp * rows + place % rowp
    valid = (place % rowp < rows)[None, :] & (position[None, :] < lengths[:, None])
    key_bias = jnp.where(valid, 0.0, -1e30).astype(fl).reshape(both, 1)
    own_valid = lax.dynamic_slice_in_dim(valid, where * rowp, rowp, 1)[:, :, None]

    x_own = pad_to(jnp.transpose(inputs, (1, 0, 2)), 1, rowp)
    dy_own = pad_to(jnp.transpose(cotangent, (1, 0, 2)), 1, rowp) * own_valid.astype(bf)
    x_all = all_blocks(x_own, where, parts).reshape(both, width)
    dy_all = all_blocks(dy_own, where, parts).reshape(both, width)

    xn1 = normalize(x_all.astype(fl), ln_gain[0], ln_bias[0]).astype(bf)
    bias_three = pad_to(
        jnp.stack([qv_bias[0], jnp.zeros_like(qv_bias[0]), qv_bias[1]]), 1, colp
    ).reshape(1, 3 * colp)
    qkv = (dot(xn1, full_qkv, 1, 0) + bias_three).astype(bf)

    attended, lses, joined = [], [], []
    for i in range(images):
        out, lse = attention_forward(qkv, key_bias, i, size, heads)
        attended.append(out)
        lses.append(lse)
        joined.append(jnp.concatenate([out] + from_others(out, parts), axis=1))
    joined = jnp.concatenate(joined, axis=0)
    attended_all = jnp.concatenate(attended, axis=0)

    h1 = x_all.astype(fl) + dot(joined, full_out, 1, 1) + out_bias[0]
    xn2 = normalize(h1, ln_gain[1], ln_bias[1]).astype(bf)
    pre = dot(xn2, full_up, 1, 0) + pad_to(up_bias, 0, hidp)
    act, pull = jax.vjp(gelu_tanh, pre)
    act = act.astype(bf)
    d_pre = pull(dot(dy_all, full_down, 1, 0))[0]
    grad_b1 = jnp.sum(d_pre, axis=0)
    d_pre_b = d_pre.astype(bf)

    d_h1, d_h1_b, d_att = [], [], []
    g2, c2, bo = 0.0, 0.0, 0.0
    for i in range(images):
        at = slice(i * size, (i + 1) * size)
        part = dot(d_pre_b[at], full_up, 1, 1).astype(bf)
        total = part.astype(fl)
        for other in from_others(part, parts):
            total = total + other.astype(fl)
        back, hat = normalize_back(h1[at], ln_gain[1], total)
        g2 = g2 + jnp.sum(total * hat, axis=0)
        c2 = c2 + jnp.sum(total, axis=0)
        full = dy_all[at].astype(fl) + back
        bo = bo + jnp.sum(full, axis=0)
        d_h1.append(full)
        d_h1_b.append(full.astype(bf))
        d_att.append(dot(d_h1_b[i], own_out, 1, 0).astype(bf))

    grad_up = dot(xn2, d_pre_b, 0, 0).astype(bf)
    grad_down = dot(dy_all, act, 0, 0).astype(bf)
    mlp_grads = lax.psum_scatter(
        jnp.concatenate([grad_up, grad_down], axis=1), "dp", scatter_dimension=0, tiled=True
    )

    y_part = dot(act, full_down, 1, 1).reshape(images, size, width)
    h1_own = lax.dynamic_slice_in_dim(h1.reshape(images, size, width), where * rowp, rowp, 1)
    y_own = h1_own + sum_blocks(y_part, where, parts, rowp) + out_bias[1]
    output = jnp.where(own_valid, y_own, 0.0).astype(bf)

    d_qkv = jnp.zeros((both, 3 * colp), bf)
    for i in range(images):
        d_qkv = attention_backward(
            qkv, key_bias, attended[i], d_att[i], lses[i], d_qkv, i, size, heads
        )
    sums_qkv = jnp.sum(d_qkv.astype(fl), axis=0)
    grad_qkv = dot(xn1, d_qkv, 0, 0).astype(bf)
    grad_out = dot(jnp.concatenate(d_h1_b, axis=0), attended_all, 0, 0).astype(bf)
    att_grads = lax.psum_scatter(
        jnp.concatenate([grad_qkv, grad_out], axis=1), "dp", scatter_dimension=0, tiled=True
    )

    d_xn1 = sum_blocks(dot(d_qkv, full_qkv, 1, 1).reshape(images, size, width), where, parts, rowp)
    back, hat = normalize_back(x_own.astype(fl), ln_gain[0], d_xn1)
    g1 = jnp.sum(d_xn1 * hat, axis=(0, 1))
    c1 = jnp.sum(d_xn1, axis=(0, 1))
    d_h1_own = jnp.stack([lax.dynamic_slice_in_dim(d, where * rowp, rowp, 0) for d in d_h1])
    d_inputs = (d_h1_own + back).astype(bf)

    b2 = jnp.sum(dy_own.astype(fl), axis=(0, 1))
    pair = jnp.stack([g1, g2 / parts, c1, c2 / parts, bo / parts, b2])
    pair = sum_everywhere(pair, "tensor")
    lone = jnp.concatenate([sums_qkv[:cols], sums_qkv[2 * colp : 2 * colp + cols], grad_b1[:hidden]])
    small = sum_everywhere(jnp.concatenate([pair.reshape(-1), lone]), "dp")
    pair = small[: 6 * width].reshape(6, width)
    lone = small[6 * width :]

    def own_rows(values):
        return jnp.transpose(values[:, :rows], (1, 0, 2))

    att_grads = att_grads.astype(fl)
    mlp_grads = mlp_grads.astype(fl)
    return (
        own_rows(output),
        own_rows(d_inputs),
        pair[0:2],
        pair[2:4],
        att_grads[:, : 3 * colp].reshape(here, 3, colp)[:, :, :cols],
        lone[: 2 * cols].reshape(2, cols),
        att_grads[:, 3 * colp : 3 * colp + cols].T,
        pair[4:6],
        mlp_grads[:, :hidden],
        lone[2 * cols :],
        mlp_grads[:, hidp : hidp + hidden].T,
    )


def solution(mesh):
    return jax.shard_map(
        on_device,
        mesh=mesh,
        in_specs=(
            P("tensor", "dp", None),
            P("dp"),
            P("tensor", "dp", None),
            P(),
            P(),
            P("dp", None, "tensor"),
            P(None, "tensor"),
            P("tensor", "dp"),
            P(),
            P("dp", "tensor"),
            P("tensor"),
            P("tensor", "dp"),
        ),
        out_specs=(
            P("tensor", "dp", None),
            P("tensor", "dp", None),
            P(),
            P(),
            P("dp", None, "tensor"),
            P(None, "tensor"),
            P("tensor", "dp"),
            P(),
            P("dp", "tensor"),
            P("tensor"),
            P("tensor", "dp"),
        ),
        check_vma=False,
    )
```

```python
import functools

import jax
import jax.numpy as jnp
from jax import lax
from jax.experimental import pallas as pl
from jax.experimental.pallas import tpu as pltpu
from jax.sharding import PartitionSpec as P


HD = 72
epsilon = 1e-06
fl = jnp.float32
bf = jnp.bfloat16


def up_to(n, m):
    return -(-n // m) * m


def dot(a, b, ca, cb):
    return lax.dot_general(a, b, (((ca,), (cb,)), ((), ())), preferred_element_type=fl)


def normalize(values, gain, shift):
    mean = jnp.mean(values, axis=-1, keepdims=True)
    centred = values - mean
    variance = jnp.mean(centred * centred, axis=-1, keepdims=True)
    return centred * lax.rsqrt(variance + epsilon) * gain + shift


def normalize_back(values, gain, grad):
    mean = jnp.mean(values, axis=-1, keepdims=True)
    centred = values - mean
    variance = jnp.mean(centred * centred, axis=-1, keepdims=True)
    inverse = lax.rsqrt(variance + epsilon)
    hat = centred * inverse
    scaled = grad * gain
    first = jnp.mean(scaled, axis=-1, keepdims=True)
    second = jnp.mean(scaled * hat, axis=-1, keepdims=True)
    return inverse * (scaled - first - hat * second), hat


def window(head, colp, win):
    start = jnp.minimum(head * HD // 128 * 128, colp - win)
    return pl.multiple_of(start, 128), head * HD - start


def forward_kernel(bias_ref, qkv_ref, out_ref, lse_ref, *, heads, colp, win):
    scale = HD ** (-0.5)
    out_ref[...] = jnp.zeros_like(out_ref)

    def one_head(head, carry):
        at, off = window(head, colp, win)
        lane = lax.broadcasted_iota(jnp.int32, (1, win), 1)
        mine = (lane >= off) & (lane < off + HD)
        query = qkv_ref[:, pl.ds(at, win)]
        keys = qkv_ref[:, pl.ds(pl.multiple_of(colp + at, 128), win)]
        values = qkv_ref[:, pl.ds(pl.multiple_of(2 * colp + at, 128), win)]
        keys = jnp.where(mine, keys, jnp.zeros_like(keys))
        values = jnp.where(mine, values, jnp.zeros_like(values))
        raw = dot(keys, query, 1, 1) * scale + bias_ref[...]
        top = jnp.max(raw, axis=0, keepdims=True)
        weights = jnp.exp(raw - top)
        total = jnp.sum(weights, axis=0, keepdims=True)
        result = dot(values, weights.astype(bf), 0, 0) / total
        lse_ref[pl.ds(head, 1), :] = top + jnp.log(total)
        out_ref[:, pl.ds(at, win)] = out_ref[:, pl.ds(at, win)] + result.T.astype(bf)
        return carry

    lax.fori_loop(0, heads, one_head, 0)


def attention_forward(qkv, bias, image, size, heads):
    colp = qkv.shape[1] // 3
    win = min(256, colp)
    return pl.pallas_call(
        functools.partial(forward_kernel, heads=heads, colp=colp, win=win),
        grid=(1,),
        out_shape=(
            jax.ShapeDtypeStruct((size, colp), bf),
            jax.ShapeDtypeStruct((heads, size), fl),
        ),
        in_specs=[
            pl.BlockSpec((size, 1), lambda g: (image, 0)),
            pl.BlockSpec((size, 3 * colp), lambda g: (image, 0)),
        ],
        out_specs=(
            pl.BlockSpec((size, colp), lambda g: (0, 0)),
            pl.BlockSpec((heads, size), lambda g: (0, 0)),
        ),
        compiler_params=pltpu.CompilerParams(vmem_limit_bytes=56 * 2**20),
        cost_estimate=pl.CostEstimate(
            flops=4 * heads * size * size * win,
            bytes_accessed=8 * size * colp,
            transcendentals=heads * size * size,
        ),
        name="attention_forward",
    )(bias, qkv)


def backward_kernel(
    bias_ref, qkv_ref, out_ref, dout_ref, lse_ref, *refs, heads, colp, win
):
    dqkv_ref = refs[-1]
    scale = HD ** (-0.5)
    dqkv_ref[...] = jnp.zeros_like(dqkv_ref)

    def one_head(head, carry):
        at, off = window(head, colp, win)
        at_k = pl.multiple_of(colp + at, 128)
        at_v = pl.multiple_of(2 * colp + at, 128)
        lane = lax.broadcasted_iota(jnp.int32, (1, win), 1)
        mine = (lane >= off) & (lane < off + HD)

        def keep(block):
            return jnp.where(mine, block, jnp.zeros_like(block))

        query = keep(qkv_ref[:, pl.ds(at, win)])
        keys = keep(qkv_ref[:, pl.ds(at_k, win)])
        values = keep(qkv_ref[:, pl.ds(at_v, win)])
        d_out = keep(dout_ref[:, pl.ds(at, win)])
        product = d_out.astype(fl) * out_ref[:, pl.ds(at, win)].astype(fl)
        delta = jnp.sum(product, axis=1, keepdims=True).T
        raw = dot(keys, query, 1, 1) * scale + bias_ref[...]
        probs = jnp.exp(raw - lse_ref[pl.ds(head, 1), :])
        d_probs = dot(values, d_out, 1, 1)
        d_raw = (probs * ((d_probs - delta) * scale)).astype(bf)

        def add(place, block):
            dqkv_ref[:, pl.ds(place, win)] = dqkv_ref[:, pl.ds(place, win)] + block.astype(bf)

        add(at_v, dot(probs.astype(bf), d_out, 1, 0))
        add(at_k, dot(d_raw, query, 1, 0))
        add(at, dot(keys, d_raw, 0, 0).T)
        return carry

    lax.fori_loop(0, heads, one_head, 0)


def attention_backward(qkv, bias, attended, d_attended, lse, old, image, size, heads):
    colp = qkv.shape[1] // 3
    win = min(256, colp)
    return pl.pallas_call(
        functools.partial(backward_kernel, heads=heads, colp=colp, win=win),
        grid=(1,),
        out_shape=jax.ShapeDtypeStruct(qkv.shape, bf),
        in_specs=[
            pl.BlockSpec((size, 1), lambda g: (image, 0)),
            pl.BlockSpec((size, 3 * colp), lambda g: (image, 0)),
            pl.BlockSpec((size, colp), lambda g: (0, 0)),
            pl.BlockSpec((size, colp), lambda g: (0, 0)),
            pl.BlockSpec((heads, size), lambda g: (0, 0)),
        ]
        + [pl.BlockSpec(memory_space=pl.ANY)] * len(old),
        out_specs=pl.BlockSpec((size, 3 * colp), lambda g: (image, 0)),
        input_output_aliases={5 + k: k for k in range(len(old))},
        compiler_params=pltpu.CompilerParams(vmem_limit_bytes=56 * 2**20),
        cost_estimate=pl.CostEstimate(
            flops=10 * heads * size * size * win,
            bytes_accessed=16 * size * colp,
            transcendentals=heads * size * size,
        ),
        name="attention_backward",
    )(bias, qkv, attended, d_attended, lse, *old)


def mlp_kernel(xn_ref, dy_ref, up_ref, down_ref, bias_ref, *refs):
    act_ref, dpre_ref, sum_ref, y_ref, dxn_ref, y_acc, dxn_acc = refs[-7:]
    step = pl.program_id(0)
    root = (2.0 / jnp.pi) ** 0.5

    @pl.when(step == 0)
    def _():
        y_acc[...] = jnp.zeros_like(y_acc)
        dxn_acc[...] = jnp.zeros_like(dxn_acc)

    up, down = up_ref[...], down_ref[...]
    pre = dot(xn_ref[...], up, 1, 0) + bias_ref[...]
    d_act = dot(dy_ref[...], down, 1, 0)
    square = pre * pre
    tanh = jnp.tanh(pre * (root + root * 0.044715 * square))
    half = 0.5 + 0.5 * tanh
    slope = half + (pre * (0.5 - 0.5 * tanh * tanh)) * (root + 3.0 * root * 0.044715 * square)
    d_pre = d_act * slope
    sum_ref[...] = jnp.sum(d_pre, axis=0, keepdims=True)
    act = (pre * half).astype(bf)
    d_pre = d_pre.astype(bf)
    act_ref[...] = act
    dpre_ref[...] = d_pre
    y_acc[...] += dot(act, down, 1, 1)
    dxn_acc[...] += dot(d_pre, up, 1, 1)

    @pl.when(step == pl.num_programs(0) - 1)
    def _():
        y_ref[...] = y_acc[...].astype(bf)
        dxn_ref[...] = dxn_acc[...].astype(bf)


def mlp(xn, dy, weights, bias, old, image, size, tile):
    both, width = xn.shape
    hidp = bias.shape[1]
    steps = hidp // tile
    rows = pl.BlockSpec((size, width), lambda g: (image, 0))
    wide = pl.BlockSpec((size, tile), lambda g: (image, g))
    whole = pl.BlockSpec((size, width), lambda g: (0, 0))
    return pl.pallas_call(
        mlp_kernel,
        grid=(steps,),
        out_shape=(
            jax.ShapeDtypeStruct((both, hidp), bf),
            jax.ShapeDtypeStruct((both, hidp), bf),
            jax.ShapeDtypeStruct((1, hidp), fl),
            jax.ShapeDtypeStruct((size, width), bf),
            jax.ShapeDtypeStruct((size, width), bf),
        ),
        in_specs=[
            rows,
            rows,
            pl.BlockSpec((width, tile), lambda g: (0, g)),
            pl.BlockSpec((width, tile), lambda g: (0, steps + g)),
            pl.BlockSpec((1, tile), lambda g: (0, g)),
        ]
        + [pl.BlockSpec(memory_space=pl.ANY)] * len(old),
        out_specs=(wide, wide, pl.BlockSpec((1, tile), lambda g: (0, g)), whole, whole),
        scratch_shapes=[pltpu.VMEM((size, width), fl)] * 2,
        input_output_aliases={5 + k: k for k in range(len(old))},
        compiler_params=pltpu.CompilerParams(vmem_limit_bytes=56 * 2**20),
        cost_estimate=pl.CostEstimate(
            flops=8 * size * width * hidp,
            bytes_accessed=4 * width * (hidp + 2 * size) + 4 * size * hidp,
            transcendentals=size * hidp,
        ),
        name="mlp",
    )(xn, dy, weights, weights, bias, *old)


def from_others(values, parts):
    return [
        lax.ppermute(values, "tensor", [((j + k) % parts, j) for j in range(parts)])
        for k in range(1, parts)
    ]


def all_blocks(values, where, parts):
    images, rows, width = values.shape
    got = [values] + from_others(values, parts)
    full = jnp.zeros((images, rows * parts, width), values.dtype)
    for k, block in enumerate(got):
        start = (where + k) % parts * rows
        full = lax.dynamic_update_slice(full, block, (jnp.int32(0), start, jnp.int32(0)))
    return full


def sum_blocks(values, where, parts, rows):
    def block(k):
        return lax.dynamic_slice_in_dim(values, (where + k) % parts * rows, rows, 1)

    total = block(0)
    for k in range(1, parts):
        pairs = [(j, (j + k) % parts) for j in range(parts)]
        total = total + lax.ppermute(block(k).astype(bf), "tensor", pairs).astype(fl)
    return total


def sum_everywhere(values, axis):
    size = lax.axis_size(axis)
    if size & (size - 1):
        return lax.psum(values, axis)
    step = 1
    while step < size:
        values = values + lax.ppermute(values, axis, [(j, j ^ step) for j in range(size)])
        step *= 2
    return values


def after(values, *others):
    return lax.optimization_barrier((values, others))[0]


def transposed(values):
    return dot(values, jnp.eye(values.shape[0], dtype=values.dtype), 0, 0)


def on_device(
    inputs,
    lengths,
    cotangent,
    ln_gain,
    ln_bias,
    w_qkv,
    qv_bias,
    w_out,
    out_bias,
    w_up,
    up_bias,
    w_down,
):
    rows, images, width = inputs.shape
    parts = lax.axis_size("tensor")
    where = lax.axis_index("tensor")
    cols = w_qkv.shape[2]
    hidden = up_bias.shape[0]
    heads = cols // HD
    here = w_qkv.shape[0]
    rowp, colp, hids, hidp = up_to(rows, 16), up_to(cols, 128), up_to(hidden, 128), up_to(hidden, 256)
    tile = next(256 * k for k in (3, 2, 1) if hidp % (256 * k) == 0)
    size = rowp * parts
    both = images * size

    def pad_to(values, axis, n):
        widths = [(0, 0)] * values.ndim
        widths[axis] = (0, n - values.shape[axis])
        return jnp.pad(values, widths)

    x_own = pad_to(jnp.transpose(inputs, (1, 0, 2)), 1, rowp)
    x_all = all_blocks(x_own, where, parts).reshape(both, width)

    shard_qkv = pad_to(w_qkv, 2, colp).reshape(here, 3 * colp)
    full_qkv = lax.all_gather(shard_qkv, "dp", axis=0, tiled=True)
    shard_out = pad_to(w_out.T, 1, colp)
    shard_out = jnp.concatenate([shard_out] + from_others(shard_out, parts), axis=1)
    shard_rest = jnp.concatenate(
        [pad_to(w_up, 1, hidp), pad_to(w_down.T, 1, hidp), shard_out], axis=1
    )
    full_rest = lax.all_gather(shard_rest, "dp", axis=0, tiled=True)
    full_out = full_rest[:, 2 * hidp :]
    own_out = full_rest[:, 2 * hidp : 2 * hidp + colp]

    place = jnp.arange(size, dtype=jnp.int32)
    position = place // rowp * rows + place % rowp
    valid = (place % rowp < rows)[None, :] & (position[None, :] < lengths[:, None])
    key_bias = jnp.where(valid, 0.0, -1e30).astype(fl).reshape(both, 1)
    own_valid = lax.dynamic_slice_in_dim(valid, where * rowp, rowp, 1)[:, :, None]

    dy_own = pad_to(jnp.transpose(cotangent, (1, 0, 2)), 1, rowp) * own_valid.astype(bf)
    dy_all = all_blocks(dy_own, where, parts).reshape(both, width)

    xn1 = normalize(x_all.astype(fl), ln_gain[0], ln_bias[0]).astype(bf)
    bias_three = pad_to(
        jnp.stack([qv_bias[0], jnp.zeros_like(qv_bias[0]), qv_bias[1]]), 1, colp
    ).reshape(1, 3 * colp)
    qkv = (dot(xn1, full_qkv, 1, 0) + bias_three).astype(bf)

    attended, lses, joined = [], [], []
    for i in range(images):
        out, lse = attention_forward(qkv, key_bias, i, size, heads)
        attended.append(out)
        lses.append(lse)
        joined.append(jnp.concatenate([out] + from_others(out, parts), axis=1))
    joined = jnp.concatenate(joined, axis=0)
    attended_all = jnp.concatenate(attended, axis=0)

    h1 = x_all.astype(fl) + dot(joined, full_out, 1, 1) + out_bias[0]
    xn2 = normalize(h1, ln_gain[1], ln_bias[1]).astype(bf)
    bias_up = pad_to(up_bias, 0, hidp)[None]
    wide, y_parts, dxn_parts, received, grad_b1 = (), [], [], [], 0.0
    for i in range(images):
        act, d_pre, sums, y_part, dxn = mlp(xn2, dy_all, full_rest, bias_up, wide, i, size, tile)
        wide = (act, d_pre)
        grad_b1 = grad_b1 + sums[0]
        y_parts.append(y_part)
        dxn_parts.append(dxn)
        received.append(from_others(dxn, parts))
    grad_up = dot(xn2, d_pre[:, :hids], 0, 0).astype(bf)
    grad_down = dot(dy_all, act[:, :hids], 0, 0).astype(bf)
    mlp_grads = jnp.concatenate([grad_up, grad_down], axis=1)
    mlp_sums = lax.psum_scatter(mlp_grads, "dp", scatter_dimension=0, tiled=True)

    d_h1, d_h1_b, d_qkv = [], [], ()
    g2, c2, bo = 0.0, 0.0, 0.0
    for i in range(images):
        at = slice(i * size, (i + 1) * size)
        got = after(received[i], mlp_grads, *d_qkv)
        total = dxn_parts[i].astype(fl)
        for other in got:
            total = total + other.astype(fl)
        back, hat = normalize_back(h1[at], ln_gain[1], total)
        g2 = g2 + jnp.sum(total * hat, axis=0)
        c2 = c2 + jnp.sum(total, axis=0)
        full = dy_all[at].astype(fl) + back
        bo = bo + jnp.sum(full, axis=0)
        d_h1.append(full)
        d_h1_b.append(full.astype(bf))
        d_att = dot(d_h1_b[i], own_out, 1, 0).astype(bf)
        d_qkv = (
            attention_backward(qkv, key_bias, attended[i], d_att, lses[i], d_qkv, i, size, heads),
        )
    (d_qkv,) = d_qkv

    y_all = after(jnp.stack(y_parts), got)
    h1_own = lax.dynamic_slice_in_dim(h1.reshape(images, size, width), where * rowp, rowp, 1)
    y_own = h1_own + sum_blocks(y_all, where, parts, rowp) + out_bias[1]
    output = jnp.where(own_valid, y_own, 0.0).astype(bf)

    grad_qkv = dot(xn1, d_qkv, 0, 0).astype(bf)
    grad_out = dot(jnp.concatenate(d_h1_b, axis=0), attended_all, 0, 0).astype(bf)
    att_grads = jnp.concatenate([grad_qkv, grad_out], axis=1)
    att_sums = lax.psum_scatter(att_grads, "dp", scatter_dimension=0, tiled=True)

    d_qkv = after(d_qkv, att_grads)
    sums_qkv = jnp.sum(d_qkv.astype(fl), axis=0)
    d_xn1 = dot(d_qkv, full_qkv, 1, 1).astype(bf).reshape(images, size, width)
    d_xn1 = sum_blocks(d_xn1, where, parts, rowp)
    back, hat = normalize_back(x_own.astype(fl), ln_gain[0], d_xn1)
    g1 = jnp.sum(d_xn1 * hat, axis=(0, 1))
    c1 = jnp.sum(d_xn1, axis=(0, 1))
    d_h1_own = jnp.stack([lax.dynamic_slice_in_dim(d, where * rowp, rowp, 0) for d in d_h1])
    d_inputs = (d_h1_own + back).astype(bf)

    b2 = jnp.sum(dy_own.astype(fl), axis=(0, 1))
    pair = jnp.stack([g1, g2 / parts, c1, c2 / parts, bo / parts, b2])
    pair = sum_everywhere(pair, "tensor")
    lone = jnp.concatenate([sums_qkv[:cols], sums_qkv[2 * colp : 2 * colp + cols], grad_b1[:hidden]])
    small = sum_everywhere(jnp.concatenate([pair.reshape(-1), lone]), "dp")
    pair = small[: 6 * width].reshape(6, width)
    lone = small[6 * width :]

    def own_rows(values):
        return jnp.transpose(values[:, :rows], (1, 0, 2))

    return (
        own_rows(output),
        own_rows(d_inputs),
        pair[0:2],
        pair[2:4],
        att_sums[:, : 3 * colp].reshape(here, 3, colp)[:, :, :cols].astype(fl),
        lone[: 2 * cols].reshape(2, cols),
        transposed(att_sums[:, 3 * colp : 3 * colp + cols]),
        pair[4:6],
        mlp_sums[:, :hidden].astype(fl),
        lone[2 * cols :],
        transposed(mlp_sums[:, hids : hids + hidden]),
    )


def solution(mesh):
    return jax.shard_map(
        on_device,
        mesh=mesh,
        in_specs=(
            P("tensor", "dp", None),
            P("dp"),
            P("tensor", "dp", None),
            P(),
            P(),
            P("dp", None, "tensor"),
            P(None, "tensor"),
            P("tensor", "dp"),
            P(),
            P("dp", "tensor"),
            P("tensor"),
            P("tensor", "dp"),
        ),
        out_specs=(
            P("tensor", "dp", None),
            P("tensor", "dp", None),
            P(),
            P(),
            P("dp", None, "tensor"),
            P(None, "tensor"),
            P("tensor", "dp"),
            P(),
            P("dp", "tensor"),
            P("tensor"),
            P("tensor", "dp"),
        ),
        check_vma=False,
    )
```

```python
import functools

import jax
import jax.numpy as jnp
from jax import lax
from jax.experimental import pallas as pl
from jax.experimental.pallas import tpu as pltpu
from jax.sharding import PartitionSpec as P


HD = 72
epsilon = 1e-06
fl = jnp.float32
bf = jnp.bfloat16


def up_to(n, m):
    return -(-n // m) * m


def dot(a, b, ca, cb):
    return lax.dot_general(a, b, (((ca,), (cb,)), ((), ())), preferred_element_type=fl)


def normalize(values, gain, shift):
    mean = jnp.mean(values, axis=-1, keepdims=True)
    centred = values - mean
    variance = jnp.mean(centred * centred, axis=-1, keepdims=True)
    return centred * lax.rsqrt(variance + epsilon) * gain + shift


def normalize_back(values, gain, grad):
    mean = jnp.mean(values, axis=-1, keepdims=True)
    centred = values - mean
    variance = jnp.mean(centred * centred, axis=-1, keepdims=True)
    inverse = lax.rsqrt(variance + epsilon)
    hat = centred * inverse
    scaled = grad * gain
    first = jnp.mean(scaled, axis=-1, keepdims=True)
    second = jnp.mean(scaled * hat, axis=-1, keepdims=True)
    return inverse * (scaled - first - hat * second), hat


def window(head, colp, win):
    start = jnp.minimum(head * HD // 128 * 128, colp - win)
    return pl.multiple_of(start, 128), head * HD - start


def forward_kernel(bias_ref, qkv_ref, out_ref, lse_ref, *, heads, colp, win):
    scale = HD ** (-0.5)
    out_ref[...] = jnp.zeros_like(out_ref)

    def one_head(head, carry):
        at, off = window(head, colp, win)
        lane = lax.broadcasted_iota(jnp.int32, (1, win), 1)
        mine = (lane >= off) & (lane < off + HD)
        query = qkv_ref[:, pl.ds(at, win)]
        keys = qkv_ref[:, pl.ds(pl.multiple_of(colp + at, 128), win)]
        values = qkv_ref[:, pl.ds(pl.multiple_of(2 * colp + at, 128), win)]
        keys = jnp.where(mine, keys, jnp.zeros_like(keys))
        values = jnp.where(mine, values, jnp.zeros_like(values))
        raw = dot(keys, query, 1, 1) * scale + bias_ref[...]
        top = jnp.max(raw, axis=0, keepdims=True)
        weights = jnp.exp(raw - top)
        total = jnp.sum(weights, axis=0, keepdims=True)
        result = dot(values, weights.astype(bf), 0, 0) / total
        lse_ref[pl.ds(head, 1), :] = top + jnp.log(total)
        out_ref[:, pl.ds(at, win)] = out_ref[:, pl.ds(at, win)] + result.T.astype(bf)
        return carry

    lax.fori_loop(0, heads, one_head, 0)


def attention_forward(qkv, bias, image, size, heads):
    colp = qkv.shape[1] // 3
    win = min(256, colp)
    return pl.pallas_call(
        functools.partial(forward_kernel, heads=heads, colp=colp, win=win),
        grid=(1,),
        out_shape=(
            jax.ShapeDtypeStruct((size, colp), bf),
            jax.ShapeDtypeStruct((heads, size), fl),
        ),
        in_specs=[
            pl.BlockSpec((size, 1), lambda g: (image, 0)),
            pl.BlockSpec((size, 3 * colp), lambda g: (image, 0)),
        ],
        out_specs=(
            pl.BlockSpec((size, colp), lambda g: (0, 0)),
            pl.BlockSpec((heads, size), lambda g: (0, 0)),
        ),
        compiler_params=pltpu.CompilerParams(vmem_limit_bytes=56 * 2**20),
        cost_estimate=pl.CostEstimate(
            flops=4 * heads * size * size * win,
            bytes_accessed=8 * size * colp,
            transcendentals=heads * size * size,
        ),
        name="attention_forward",
    )(bias, qkv)


def backward_kernel(
    bias_ref, qkv_ref, out_ref, dout_ref, lse_ref, *refs, heads, colp, win
):
    dqkv_ref = refs[-1]
    scale = HD ** (-0.5)
    dqkv_ref[...] = jnp.zeros_like(dqkv_ref)

    def one_head(head, carry):
        at, off = window(head, colp, win)
        at_k = pl.multiple_of(colp + at, 128)
        at_v = pl.multiple_of(2 * colp + at, 128)
        lane = lax.broadcasted_iota(jnp.int32, (1, win), 1)
        mine = (lane >= off) & (lane < off + HD)

        def keep(block):
            return jnp.where(mine, block, jnp.zeros_like(block))

        query = keep(qkv_ref[:, pl.ds(at, win)])
        keys = keep(qkv_ref[:, pl.ds(at_k, win)])
        values = keep(qkv_ref[:, pl.ds(at_v, win)])
        d_out = keep(dout_ref[:, pl.ds(at, win)])
        product = d_out.astype(fl) * out_ref[:, pl.ds(at, win)].astype(fl)
        delta = jnp.sum(product, axis=1, keepdims=True).T
        raw = dot(keys, query, 1, 1) * scale + bias_ref[...]
        probs = jnp.exp(raw - lse_ref[pl.ds(head, 1), :])
        d_probs = dot(values, d_out, 1, 1)
        d_raw = (probs * ((d_probs - delta) * scale)).astype(bf)

        def add(place, block):
            dqkv_ref[:, pl.ds(place, win)] = dqkv_ref[:, pl.ds(place, win)] + block.astype(bf)

        add(at_v, dot(probs.astype(bf), d_out, 1, 0))
        add(at_k, dot(d_raw, query, 1, 0))
        add(at, dot(keys, d_raw, 0, 0).T)
        return carry

    lax.fori_loop(0, heads, one_head, 0)


def attention_backward(qkv, bias, attended, d_attended, lse, old, image, size, heads):
    colp = qkv.shape[1] // 3
    win = min(256, colp)
    return pl.pallas_call(
        functools.partial(backward_kernel, heads=heads, colp=colp, win=win),
        grid=(1,),
        out_shape=jax.ShapeDtypeStruct(qkv.shape, bf),
        in_specs=[
            pl.BlockSpec((size, 1), lambda g: (image, 0)),
            pl.BlockSpec((size, 3 * colp), lambda g: (image, 0)),
            pl.BlockSpec((size, colp), lambda g: (0, 0)),
            pl.BlockSpec((size, colp), lambda g: (0, 0)),
            pl.BlockSpec((heads, size), lambda g: (0, 0)),
        ]
        + [pl.BlockSpec(memory_space=pl.ANY)] * len(old),
        out_specs=pl.BlockSpec((size, 3 * colp), lambda g: (image, 0)),
        input_output_aliases={5 + k: k for k in range(len(old))},
        compiler_params=pltpu.CompilerParams(vmem_limit_bytes=56 * 2**20),
        cost_estimate=pl.CostEstimate(
            flops=10 * heads * size * size * win,
            bytes_accessed=16 * size * colp,
            transcendentals=heads * size * size,
        ),
        name="attention_backward",
    )(bias, qkv, attended, d_attended, lse, *old)


def mlp_kernel(xn_ref, dy_ref, up_ref, down_ref, bias_ref, *refs):
    act_ref, dpre_ref, sum_ref, y_ref, dxn_ref, y_acc, dxn_acc = refs[-7:]
    step = pl.program_id(0)
    root = (2.0 / jnp.pi) ** 0.5

    @pl.when(step == 0)
    def _():
        y_acc[...] = jnp.zeros_like(y_acc)
        dxn_acc[...] = jnp.zeros_like(dxn_acc)

    up, down = up_ref[...], down_ref[...]
    pre = dot(xn_ref[...], up, 1, 0) + bias_ref[...]
    d_act = dot(dy_ref[...], down, 1, 0)
    square = pre * pre
    tanh = jnp.tanh(pre * (root + root * 0.044715 * square))
    half = 0.5 + 0.5 * tanh
    slope = half + (pre * (0.5 - 0.5 * tanh * tanh)) * (root + 3.0 * root * 0.044715 * square)
    d_pre = d_act * slope
    sum_ref[...] = jnp.sum(d_pre, axis=0, keepdims=True)
    act = (pre * half).astype(bf)
    d_pre = d_pre.astype(bf)
    act_ref[...] = act
    dpre_ref[...] = d_pre
    y_acc[...] += dot(act, down, 1, 1)
    dxn_acc[...] += dot(d_pre, up, 1, 1)

    @pl.when(step == pl.num_programs(0) - 1)
    def _():
        y_ref[...] = y_acc[...].astype(bf)
        dxn_ref[...] = dxn_acc[...].astype(bf)


def mlp(xn, dy, weights, bias, old, image, size, tile):
    both, width = xn.shape
    hidp = bias.shape[1]
    steps = hidp // tile
    rows = pl.BlockSpec((size, width), lambda g: (image, 0))
    wide = pl.BlockSpec((size, tile), lambda g: (image, g))
    whole = pl.BlockSpec((size, width), lambda g: (0, 0))
    return pl.pallas_call(
        mlp_kernel,
        grid=(steps,),
        out_shape=(
            jax.ShapeDtypeStruct((both, hidp), bf),
            jax.ShapeDtypeStruct((both, hidp), bf),
            jax.ShapeDtypeStruct((1, hidp), fl),
            jax.ShapeDtypeStruct((size, width), bf),
            jax.ShapeDtypeStruct((size, width), bf),
        ),
        in_specs=[
            rows,
            rows,
            pl.BlockSpec((width, tile), lambda g: (0, g)),
            pl.BlockSpec((width, tile), lambda g: (0, steps + g)),
            pl.BlockSpec((1, tile), lambda g: (0, g)),
        ]
        + [pl.BlockSpec(memory_space=pl.ANY)] * len(old),
        out_specs=(wide, wide, pl.BlockSpec((1, tile), lambda g: (0, g)), whole, whole),
        scratch_shapes=[pltpu.VMEM((size, width), fl)] * 2,
        input_output_aliases={5 + k: k for k in range(len(old))},
        compiler_params=pltpu.CompilerParams(vmem_limit_bytes=56 * 2**20),
        cost_estimate=pl.CostEstimate(
            flops=8 * size * width * hidp,
            bytes_accessed=4 * width * (hidp + 2 * size) + 4 * size * hidp,
            transcendentals=size * hidp,
        ),
        name="mlp",
    )(xn, dy, weights, weights, bias, *old)


def from_others(values, parts):
    return [
        lax.ppermute(values, "tensor", [((j + k) % parts, j) for j in range(parts)])
        for k in range(1, parts)
    ]


def all_blocks(values, got, where):
    images, rows, width = values.shape
    got = [values] + got
    parts = len(got)
    full = jnp.zeros((images, rows * parts, width), values.dtype)
    for k, block in enumerate(got):
        start = (where + k) % parts * rows
        full = lax.dynamic_update_slice(full, block, (jnp.int32(0), start, jnp.int32(0)))
    return full


def sum_blocks(values, where, parts, rows):
    def block(k):
        return lax.dynamic_slice_in_dim(values, (where + k) % parts * rows, rows, 1)

    total = block(0)
    for k in range(1, parts):
        pairs = [(j, (j + k) % parts) for j in range(parts)]
        total = total + lax.ppermute(block(k).astype(bf), "tensor", pairs).astype(fl)
    return total


def gather_by_halves(values, axis):
    size = lax.axis_size(axis)
    rows, width = values.shape
    if size & (size - 1):
        return lax.all_gather(values, axis, axis=0, tiled=True)
    have = values[None]
    step = size // 2
    while step:
        got = lax.ppermute(have, axis, [(j, j ^ step) for j in range(size)])
        first = lax.axis_index(axis) // step % 2 == 0
        low, high = jnp.where(first, have, got), jnp.where(first, got, have)
        have = jnp.stack([low, high], axis=1).reshape(-1, rows, width)
        step //= 2
    return have.reshape(-1, width)


def exchange_half(values, axis, step):
    size = lax.axis_size(axis)
    blocks, rows, width = values.shape
    split = values.reshape(blocks // 2, 2, rows, width)
    mine = lax.axis_index(axis) // step % 2
    send = lax.dynamic_index_in_dim(split, 1 - mine, 1, False)
    keep = lax.dynamic_index_in_dim(split, mine, 1, False)
    return keep, lax.ppermute(send, axis, [(j, j ^ step) for j in range(size)])


def sum_everywhere(values, axis):
    size = lax.axis_size(axis)
    if size & (size - 1):
        return lax.psum(values, axis)
    step = 1
    while step < size:
        values = values + lax.ppermute(values, axis, [(j, j ^ step) for j in range(size)])
        step *= 2
    return values


def after(values, *others):
    return lax.optimization_barrier((values, others))[0]


def transposed(values):
    return dot(values, jnp.eye(values.shape[0], dtype=values.dtype), 0, 0)


def on_device(
    inputs,
    lengths,
    cotangent,
    ln_gain,
    ln_bias,
    w_qkv,
    qv_bias,
    w_out,
    out_bias,
    w_up,
    up_bias,
    w_down,
):
    rows, images, width = inputs.shape
    parts = lax.axis_size("tensor")
    where = lax.axis_index("tensor")
    cols = w_qkv.shape[2]
    hidden = up_bias.shape[0]
    heads = cols // HD
    here = w_qkv.shape[0]
    rowp, colp, hids, hidp = up_to(rows, 16), up_to(cols, 128), up_to(hidden, 128), up_to(hidden, 256)
    tile = next(256 * k for k in (3, 2, 1) if hidp % (256 * k) == 0)
    size = rowp * parts
    both = images * size

    def pad_to(values, axis, n):
        widths = [(0, 0)] * values.ndim
        widths[axis] = (0, n - values.shape[axis])
        return jnp.pad(values, widths)

    x_own = pad_to(jnp.transpose(inputs, (1, 0, 2)), 1, rowp)
    x_all = all_blocks(x_own, from_others(x_own, parts), where).reshape(both, width)

    shard_qkv = pad_to(w_qkv, 2, colp).reshape(here, 3 * colp)
    full_qkv = lax.all_gather(shard_qkv, "dp", axis=0, tiled=True)
    shard_out = pad_to(w_out.T, 1, colp)
    shard_out = jnp.concatenate([shard_out] + from_others(shard_out, parts), axis=1)
    shard_mlp = jnp.concatenate([pad_to(w_up, 1, hidp), pad_to(w_down.T, 1, hidp)], axis=1)
    full_mlp = lax.all_gather(shard_mlp, "dp", axis=0, tiled=True)
    full_out = gather_by_halves(shard_out, "dp")
    own_out = full_out[:, :colp]

    place = jnp.arange(size, dtype=jnp.int32)
    position = place // rowp * rows + place % rowp
    valid = (place % rowp < rows)[None, :] & (position[None, :] < lengths[:, None])
    key_bias = jnp.where(valid, 0.0, -1e30).astype(fl).reshape(both, 1)
    own_valid = lax.dynamic_slice_in_dim(valid, where * rowp, rowp, 1)[:, :, None]

    dy_own = pad_to(jnp.transpose(cotangent, (1, 0, 2)), 1, rowp) * own_valid.astype(bf)
    dy_others = from_others(dy_own, parts)

    xn1 = normalize(x_all.astype(fl), ln_gain[0], ln_bias[0]).astype(bf)
    bias_three = pad_to(
        jnp.stack([qv_bias[0], jnp.zeros_like(qv_bias[0]), qv_bias[1]]), 1, colp
    ).reshape(1, 3 * colp)
    qkv = (dot(xn1, full_qkv, 1, 0) + bias_three).astype(bf)

    attended, lses, joined = [], [], []
    for i in range(images):
        out, lse = attention_forward(qkv, key_bias, i, size, heads)
        attended.append(out)
        lses.append(lse)
        joined.append(jnp.concatenate([out] + from_others(out, parts), axis=1))
    dy_others = after(dy_others, *attended)
    dy_all = all_blocks(dy_own, dy_others, where).reshape(both, width)
    joined = jnp.concatenate(joined, axis=0)
    attended_all = jnp.concatenate(attended, axis=0)

    h1 = x_all.astype(fl) + dot(joined, full_out, 1, 1) + out_bias[0]
    xn2 = normalize(h1, ln_gain[1], ln_bias[1]).astype(bf)
    bias_up = pad_to(up_bias, 0, hidp)[None]
    wide, y_parts, dxn_parts, received, grad_b1 = (), [], [], [], 0.0
    for i in range(images):
        act, d_pre, sums, y_part, dxn = mlp(
            xn2, dy_all, full_mlp, bias_up, wide, i, size, tile
        )
        wide = (act, d_pre)
        grad_b1 = grad_b1 + sums[0]
        y_parts.append(y_part)
        dxn_parts.append(dxn)
        received.append(from_others(dxn, parts))
    grad_down = dot(dy_all, act[:, :hids], 0, 0).astype(bf)
    down_sums = lax.psum_scatter(grad_down, "dp", scatter_dimension=0, tiled=True)
    down_sums = lax.optimization_barrier(down_sums)
    d_pre = after(d_pre, grad_down)
    grad_up = dot(xn2, d_pre[:, :hids], 0, 0).astype(bf)
    ring = lax.axis_size("dp")
    halving = not ring & (ring - 1)
    if halving:
        up_sums, step = grad_up.reshape(ring, here, hids), 1
        pending = exchange_half(up_sums, "dp", step)
    else:
        up_sums, step, pending = lax.psum_scatter(grad_up, "dp", tiled=True), ring, ()

    def next_half(pending, step, *others):
        if not halving or step == ring:
            return pending, step
        keep, got = pending
        if others:
            got = after(got, *others)
        total = (keep.astype(fl) + got.astype(fl)).astype(bf)
        step *= 2
        if step == ring:
            return total, step
        return exchange_half(total, "dp", step), step

    d_h1, d_h1_b, d_qkv = [], [], ()
    g2, c2, bo = 0.0, 0.0, 0.0
    for i in range(images):
        at = slice(i * size, (i + 1) * size)
        got = after(received[i], grad_up, grad_down, *d_qkv)
        total = dxn_parts[i].astype(fl)
        for other in got:
            total = total + other.astype(fl)
        back, hat = normalize_back(h1[at], ln_gain[1], total)
        g2 = g2 + jnp.sum(total * hat, axis=0)
        c2 = c2 + jnp.sum(total, axis=0)
        full = dy_all[at].astype(fl) + back
        bo = bo + jnp.sum(full, axis=0)
        d_h1.append(full)
        d_h1_b.append(full.astype(bf))
        d_att = dot(d_h1_b[i], own_out, 1, 0).astype(bf)
        d_qkv = (
            attention_backward(qkv, key_bias, attended[i], d_att, lses[i], d_qkv, i, size, heads),
        )
        pending, step = next_half(pending, step, *d_qkv)
    (d_qkv,) = d_qkv

    y_all = after(jnp.stack(y_parts), got)
    h1_own = lax.dynamic_slice_in_dim(h1.reshape(images, size, width), where * rowp, rowp, 1)
    y_own = h1_own + sum_blocks(y_all, where, parts, rowp) + out_bias[1]
    output = jnp.where(own_valid, y_own, 0.0).astype(bf)

    grad_qkv = dot(xn1, d_qkv, 0, 0).astype(bf)
    grad_out = dot(jnp.concatenate(d_h1_b, axis=0), attended_all, 0, 0).astype(bf)
    att_grads = jnp.concatenate([grad_qkv, grad_out], axis=1)
    att_sums = lax.psum_scatter(att_grads, "dp", scatter_dimension=0, tiled=True)

    pending, step = next_half(pending, step, att_grads)
    d_qkv = after(d_qkv, att_grads)
    sums_qkv = jnp.sum(d_qkv.astype(fl), axis=0)
    d_xn1 = dot(d_qkv, full_qkv, 1, 1).astype(bf).reshape(images, size, width)
    d_xn1 = sum_blocks(d_xn1, where, parts, rowp)
    back, hat = normalize_back(x_own.astype(fl), ln_gain[0], d_xn1)
    g1 = jnp.sum(d_xn1 * hat, axis=(0, 1))
    c1 = jnp.sum(d_xn1, axis=(0, 1))
    d_h1_own = jnp.stack([lax.dynamic_slice_in_dim(d, where * rowp, rowp, 0) for d in d_h1])
    d_inputs = (d_h1_own + back).astype(bf)

    b2 = jnp.sum(dy_own.astype(fl), axis=(0, 1))
    pair = jnp.stack([g1, g2 / parts, c1, c2 / parts, bo / parts, b2])
    pair = sum_everywhere(pair, "tensor")
    lone = jnp.concatenate([sums_qkv[:cols], sums_qkv[2 * colp : 2 * colp + cols], grad_b1[:hidden]])
    small = sum_everywhere(jnp.concatenate([pair.reshape(-1), lone]), "dp")
    pair = small[: 6 * width].reshape(6, width)
    lone = small[6 * width :]

    while halving and step < ring:
        pending, step = next_half(pending, step)
    if halving:
        up_sums = pending[0]

    def own_rows(values):
        return jnp.transpose(values[:, :rows], (1, 0, 2))

    return (
        own_rows(output),
        own_rows(d_inputs),
        pair[0:2],
        pair[2:4],
        att_sums[:, : 3 * colp].reshape(here, 3, colp)[:, :, :cols].astype(fl),
        lone[: 2 * cols].reshape(2, cols),
        transposed(att_sums[:, 3 * colp : 3 * colp + cols]),
        pair[4:6],
        up_sums[:, :hidden].astype(fl),
        lone[2 * cols :],
        transposed(down_sums)[:hidden],
    )


def solution(mesh):
    return jax.shard_map(
        on_device,
        mesh=mesh,
        in_specs=(
            P("tensor", "dp", None),
            P("dp"),
            P("tensor", "dp", None),
            P(),
            P(),
            P("dp", None, "tensor"),
            P(None, "tensor"),
            P("tensor", "dp"),
            P(),
            P("dp", "tensor"),
            P("tensor"),
            P("tensor", "dp"),
        ),
        out_specs=(
            P("tensor", "dp", None),
            P("tensor", "dp", None),
            P(),
            P(),
            P("dp", None, "tensor"),
            P(None, "tensor"),
            P("tensor", "dp"),
            P(),
            P("dp", "tensor"),
            P("tensor"),
            P("tensor", "dp"),
        ),
        check_vma=False,
    )
```

```python
import functools

import jax
import jax.numpy as jnp
from jax import lax
from jax.experimental import pallas as pl
from jax.experimental.pallas import tpu as pltpu
from jax.sharding import PartitionSpec as P


HD = 72
epsilon = 1e-06
fl = jnp.float32
bf = jnp.bfloat16


def up_to(n, m):
    return -(-n // m) * m


def dot(a, b, ca, cb):
    return lax.dot_general(a, b, (((ca,), (cb,)), ((), ())), preferred_element_type=fl)


def normalize(values, gain, shift):
    mean = jnp.mean(values, axis=-1, keepdims=True)
    centred = values - mean
    variance = jnp.mean(centred * centred, axis=-1, keepdims=True)
    return centred * lax.rsqrt(variance + epsilon) * gain + shift


def normalize_back(values, gain, grad):
    mean = jnp.mean(values, axis=-1, keepdims=True)
    centred = values - mean
    variance = jnp.mean(centred * centred, axis=-1, keepdims=True)
    inverse = lax.rsqrt(variance + epsilon)
    hat = centred * inverse
    scaled = grad * gain
    first = jnp.mean(scaled, axis=-1, keepdims=True)
    second = jnp.mean(scaled * hat, axis=-1, keepdims=True)
    return inverse * (scaled - first - hat * second), hat


def window(head, colp, win):
    start = jnp.minimum(head * HD // 128 * 128, colp - win)
    return pl.multiple_of(start, 128), head * HD - start


def forward_kernel(bias_ref, qkv_ref, out_ref, lse_ref, *, heads, colp, win):
    scale = HD ** (-0.5)
    out_ref[...] = jnp.zeros_like(out_ref)

    def one_head(head, carry):
        at, off = window(head, colp, win)
        lane = lax.broadcasted_iota(jnp.int32, (1, win), 1)
        mine = (lane >= off) & (lane < off + HD)
        query = qkv_ref[:, pl.ds(at, win)]
        keys = qkv_ref[:, pl.ds(pl.multiple_of(colp + at, 128), win)]
        values = qkv_ref[:, pl.ds(pl.multiple_of(2 * colp + at, 128), win)]
        keys = jnp.where(mine, keys, jnp.zeros_like(keys))
        values = jnp.where(mine, values, jnp.zeros_like(values))
        raw = dot(keys, query, 1, 1) * scale + bias_ref[...]
        top = jnp.max(raw, axis=0, keepdims=True)
        weights = jnp.exp(raw - top)
        total = jnp.sum(weights, axis=0, keepdims=True)
        result = dot(values, weights.astype(bf), 0, 0) / total
        lse_ref[pl.ds(head, 1), :] = top + jnp.log(total)
        out_ref[:, pl.ds(at, win)] = out_ref[:, pl.ds(at, win)] + result.T.astype(bf)
        return carry

    lax.fori_loop(0, heads, one_head, 0)


def attention_forward(qkv, bias, image, size, heads):
    colp = qkv.shape[1] // 3
    win = min(256, colp)
    return pl.pallas_call(
        functools.partial(forward_kernel, heads=heads, colp=colp, win=win),
        grid=(1,),
        out_shape=(
            jax.ShapeDtypeStruct((size, colp), bf),
            jax.ShapeDtypeStruct((heads, size), fl),
        ),
        in_specs=[
            pl.BlockSpec((size, 1), lambda g: (image, 0)),
            pl.BlockSpec((size, 3 * colp), lambda g: (image, 0)),
        ],
        out_specs=(
            pl.BlockSpec((size, colp), lambda g: (0, 0)),
            pl.BlockSpec((heads, size), lambda g: (0, 0)),
        ),
        compiler_params=pltpu.CompilerParams(vmem_limit_bytes=56 * 2**20),
        cost_estimate=pl.CostEstimate(
            flops=4 * heads * size * size * win,
            bytes_accessed=8 * size * colp,
            transcendentals=heads * size * size,
        ),
        name="attention_forward",
    )(bias, qkv)


def backward_kernel(
    bias_ref, qkv_ref, out_ref, dout_ref, lse_ref, *refs, heads, colp, win
):
    dqkv_ref = refs[-1]
    scale = HD ** (-0.5)
    dqkv_ref[...] = jnp.zeros_like(dqkv_ref)

    def one_head(head, carry):
        at, off = window(head, colp, win)
        at_k = pl.multiple_of(colp + at, 128)
        at_v = pl.multiple_of(2 * colp + at, 128)
        lane = lax.broadcasted_iota(jnp.int32, (1, win), 1)
        mine = (lane >= off) & (lane < off + HD)

        def keep(block):
            return jnp.where(mine, block, jnp.zeros_like(block))

        query = keep(qkv_ref[:, pl.ds(at, win)])
        keys = keep(qkv_ref[:, pl.ds(at_k, win)])
        values = keep(qkv_ref[:, pl.ds(at_v, win)])
        d_out = keep(dout_ref[:, pl.ds(at, win)])
        product = d_out.astype(fl) * out_ref[:, pl.ds(at, win)].astype(fl)
        delta = jnp.sum(product, axis=1, keepdims=True).T
        raw = dot(keys, query, 1, 1) * scale + bias_ref[...]
        probs = jnp.exp(raw - lse_ref[pl.ds(head, 1), :])
        d_probs = dot(values, d_out, 1, 1)
        d_raw = (probs * ((d_probs - delta) * scale)).astype(bf)

        def add(place, block):
            dqkv_ref[:, pl.ds(place, win)] = dqkv_ref[:, pl.ds(place, win)] + block.astype(bf)

        add(at_v, dot(probs.astype(bf), d_out, 1, 0))
        add(at_k, dot(d_raw, query, 1, 0))
        add(at, dot(keys, d_raw, 0, 0).T)
        return carry

    lax.fori_loop(0, heads, one_head, 0)


def attention_backward(qkv, bias, attended, d_attended, lse, old, image, size, heads):
    colp = qkv.shape[1] // 3
    win = min(256, colp)
    return pl.pallas_call(
        functools.partial(backward_kernel, heads=heads, colp=colp, win=win),
        grid=(1,),
        out_shape=jax.ShapeDtypeStruct(qkv.shape, bf),
        in_specs=[
            pl.BlockSpec((size, 1), lambda g: (image, 0)),
            pl.BlockSpec((size, 3 * colp), lambda g: (image, 0)),
            pl.BlockSpec((size, colp), lambda g: (0, 0)),
            pl.BlockSpec((size, colp), lambda g: (0, 0)),
            pl.BlockSpec((heads, size), lambda g: (0, 0)),
        ]
        + [pl.BlockSpec(memory_space=pl.ANY)] * len(old),
        out_specs=pl.BlockSpec((size, 3 * colp), lambda g: (image, 0)),
        input_output_aliases={5 + k: k for k in range(len(old))},
        compiler_params=pltpu.CompilerParams(vmem_limit_bytes=56 * 2**20),
        cost_estimate=pl.CostEstimate(
            flops=10 * heads * size * size * win,
            bytes_accessed=16 * size * colp,
            transcendentals=heads * size * size,
        ),
        name="attention_backward",
    )(bias, qkv, attended, d_attended, lse, *old)


def mlp_kernel(xn_ref, dy_ref, up_ref, down_ref, bias_ref, *refs):
    act_ref, dpre_ref, sum_ref, y_ref, dxn_ref, y_acc, dxn_acc = refs[-7:]
    step = pl.program_id(0)
    root = (2.0 / jnp.pi) ** 0.5

    @pl.when(step == 0)
    def _():
        y_acc[...] = jnp.zeros_like(y_acc)
        dxn_acc[...] = jnp.zeros_like(dxn_acc)

    up, down = up_ref[...], down_ref[...]
    pre = dot(xn_ref[...], up, 1, 0) + bias_ref[...]
    d_act = dot(dy_ref[...], down, 1, 0)
    square = pre * pre
    tanh = jnp.tanh(pre * (root + root * 0.044715 * square))
    half = 0.5 + 0.5 * tanh
    slope = half + (pre * (0.5 - 0.5 * tanh * tanh)) * (root + 3.0 * root * 0.044715 * square)
    d_pre = d_act * slope
    sum_ref[...] = jnp.sum(d_pre, axis=0, keepdims=True)
    act = (pre * half).astype(bf)
    d_pre = d_pre.astype(bf)
    act_ref[...] = act
    dpre_ref[...] = d_pre
    y_acc[...] += dot(act, down, 1, 1)
    dxn_acc[...] += dot(d_pre, up, 1, 1)

    @pl.when(step == pl.num_programs(0) - 1)
    def _():
        y_ref[...] = y_acc[...].astype(bf)
        dxn_ref[...] = dxn_acc[...].astype(bf)


def mlp(xn, dy, weights, bias, old, image, size, tile):
    both, width = xn.shape
    hidp = bias.shape[1]
    steps = hidp // tile
    rows = pl.BlockSpec((size, width), lambda g: (image, 0))
    wide = pl.BlockSpec((size, tile), lambda g: (image, g))
    whole = pl.BlockSpec((size, width), lambda g: (0, 0))
    return pl.pallas_call(
        mlp_kernel,
        grid=(steps,),
        out_shape=(
            jax.ShapeDtypeStruct((both, hidp), bf),
            jax.ShapeDtypeStruct((both, hidp), bf),
            jax.ShapeDtypeStruct((1, hidp), fl),
            jax.ShapeDtypeStruct((size, width), bf),
            jax.ShapeDtypeStruct((size, width), bf),
        ),
        in_specs=[
            rows,
            rows,
            pl.BlockSpec((width, tile), lambda g: (0, g)),
            pl.BlockSpec((width, tile), lambda g: (0, steps + g)),
            pl.BlockSpec((1, tile), lambda g: (0, g)),
        ]
        + [pl.BlockSpec(memory_space=pl.ANY)] * len(old),
        out_specs=(wide, wide, pl.BlockSpec((1, tile), lambda g: (0, g)), whole, whole),
        scratch_shapes=[pltpu.VMEM((size, width), fl)] * 2,
        input_output_aliases={5 + k: k for k in range(len(old))},
        compiler_params=pltpu.CompilerParams(vmem_limit_bytes=56 * 2**20),
        cost_estimate=pl.CostEstimate(
            flops=8 * size * width * hidp,
            bytes_accessed=4 * width * (hidp + 2 * size) + 4 * size * hidp,
            transcendentals=size * hidp,
        ),
        name="mlp",
    )(xn, dy, weights, weights, bias, *old)


def from_others(values, parts):
    return [
        lax.ppermute(values, "tensor", [((j + k) % parts, j) for j in range(parts)])
        for k in range(1, parts)
    ]


def all_blocks(values, got, where):
    images, rows, width = values.shape
    got = [values] + got
    parts = len(got)
    full = jnp.zeros((images, rows * parts, width), values.dtype)
    for k, block in enumerate(got):
        start = (where + k) % parts * rows
        full = lax.dynamic_update_slice(full, block, (jnp.int32(0), start, jnp.int32(0)))
    return full


def send_blocks(values, where, parts, rows):
    def block(k):
        return lax.dynamic_slice_in_dim(values, (where + k) % parts * rows, rows, 1)

    shares = [block(0)]
    for k in range(1, parts):
        pairs = [(j, (j + k) % parts) for j in range(parts)]
        shares.append(lax.ppermute(block(k), "tensor", pairs))
    return shares


def sum_of(shares):
    return functools.reduce(jnp.add, [share.astype(fl) for share in shares])


def start_doubling(have, axis, step):
    size = lax.axis_size(axis)
    return have, lax.ppermute(have, axis, [(j, j ^ step) for j in range(size)])


def end_doubling(have, got, axis, step):
    first = lax.axis_index(axis) // step % 2 == 0
    low, high = jnp.where(first, have, got), jnp.where(first, got, have)
    return jnp.stack([low, high], axis=1).reshape(-1, *have.shape[1:])


def exchange_half(values, axis, step):
    size = lax.axis_size(axis)
    blocks, rows, width = values.shape
    split = values.reshape(blocks // 2, 2, rows, width)
    mine = lax.axis_index(axis) // step % 2
    send = lax.dynamic_index_in_dim(split, 1 - mine, 1, False)
    keep = lax.dynamic_index_in_dim(split, mine, 1, False)
    return keep, lax.ppermute(send, axis, [(j, j ^ step) for j in range(size)])


def sum_everywhere(values, axis):
    size = lax.axis_size(axis)
    if size & (size - 1):
        return lax.psum(values, axis)
    step = 1
    while step < size:
        values = values + lax.ppermute(values, axis, [(j, j ^ step) for j in range(size)])
        step *= 2
    return values


def after(values, *others):
    return lax.optimization_barrier((values, others))[0]


def transposed(values):
    return dot(values, jnp.eye(values.shape[0], dtype=values.dtype), 0, 0)


def on_device(
    inputs,
    lengths,
    cotangent,
    ln_gain,
    ln_bias,
    w_qkv,
    qv_bias,
    w_out,
    out_bias,
    w_up,
    up_bias,
    w_down,
):
    rows, images, width = inputs.shape
    parts = lax.axis_size("tensor")
    where = lax.axis_index("tensor")
    cols = w_qkv.shape[2]
    hidden = up_bias.shape[0]
    heads = cols // HD
    here = w_qkv.shape[0]
    rowp, colp, hids, hidp = up_to(rows, 16), up_to(cols, 128), up_to(hidden, 128), up_to(hidden, 256)
    tile = next(256 * k for k in (3, 2, 1) if hidp % (256 * k) == 0)
    size = rowp * parts
    both = images * size

    def pad_to(values, axis, n):
        widths = [(0, 0)] * values.ndim
        widths[axis] = (0, n - values.shape[axis])
        return jnp.pad(values, widths)

    x_own = pad_to(jnp.transpose(inputs, (1, 0, 2)), 1, rowp)
    x_all = all_blocks(x_own, from_others(x_own, parts), where).reshape(both, width)

    shard_qkv = pad_to(w_qkv, 2, colp).reshape(here, 3 * colp)
    full_qkv = lax.all_gather(shard_qkv, "dp", axis=0, tiled=True)
    shard_out = pad_to(w_out.T, 1, colp)
    shard_out = jnp.concatenate([shard_out] + from_others(shard_out, parts), axis=1)
    ring = lax.axis_size("dp")
    halving = not ring & (ring - 1)
    shard_mlp = jnp.concatenate([pad_to(w_up, 1, hidp), pad_to(w_down.T, 1, hidp)], axis=1)
    full_mlp = lax.all_gather(shard_mlp, "dp", axis=0, tiled=True)

    place = jnp.arange(size, dtype=jnp.int32)
    position = place // rowp * rows + place % rowp
    valid = (place % rowp < rows)[None, :] & (position[None, :] < lengths[:, None])
    key_bias = jnp.where(valid, 0.0, -1e30).astype(fl).reshape(both, 1)
    own_valid = lax.dynamic_slice_in_dim(valid, where * rowp, rowp, 1)[:, :, None]

    dy_own = pad_to(jnp.transpose(cotangent, (1, 0, 2)), 1, rowp) * own_valid.astype(bf)
    dy_others = from_others(dy_own, parts)

    xn1 = normalize(x_all.astype(fl), ln_gain[0], ln_bias[0]).astype(bf)
    bias_three = pad_to(
        jnp.stack([qv_bias[0], jnp.zeros_like(qv_bias[0]), qv_bias[1]]), 1, colp
    ).reshape(1, 3 * colp)
    doubling = ring // 2
    if halving:
        pending = start_doubling(after(shard_out, full_qkv)[None], "dp", doubling)
    qkv = (dot(xn1, full_qkv, 1, 0) + bias_three).astype(bf)

    def next_double(pending, step, *others):
        if not halving or not step:
            return pending, step
        have, got = pending
        if others:
            got = after(got, *others)
        have = end_doubling(have, got, "dp", step)
        step //= 2
        return (start_doubling(have, "dp", step) if step else (have,)), step

    if halving:
        pending, doubling = next_double(pending, doubling, qkv)
    attended, lses, joined = [], [], []
    for i in range(images):
        out, lse = attention_forward(qkv, key_bias, i, size, heads)
        attended.append(out)
        lses.append(lse)
        if halving:
            pending, doubling = next_double(pending, doubling, out)
    attended = after(attended, *attended)
    for i in range(images):
        others = from_others(attended[i], parts)
        joined.append(jnp.concatenate([attended[i]] + others, axis=1))
    if halving:
        while doubling:
            pending, doubling = next_double(pending, doubling)
        full_out = pending[0].reshape(width, -1)
    else:
        full_out = lax.all_gather(shard_out, "dp", axis=0, tiled=True)
    own_out = full_out[:, :colp]
    dy_others = after(dy_others, *attended)
    dy_all = all_blocks(dy_own, dy_others, where).reshape(both, width)
    joined = jnp.concatenate(joined, axis=0)
    attended_all = joined[:, :colp]

    h1 = x_all.astype(fl) + dot(joined, full_out, 1, 1) + out_bias[0]
    xn2 = normalize(h1, ln_gain[1], ln_bias[1]).astype(bf)
    bias_up = pad_to(up_bias, 0, hidp)[None]
    wide, y_parts, dxn_parts, received, grad_b1 = (), [], [], [], 0.0
    for i in range(images):
        act, d_pre, sums, y_part, dxn = mlp(
            xn2, dy_all, full_mlp, bias_up, wide, i, size, tile
        )
        wide = (act, d_pre)
        grad_b1 = grad_b1 + sums[0]
        y_parts.append(y_part)
        dxn_parts.append(dxn)
        received.append(from_others(dxn, parts))
    grad_down = dot(dy_all, act[:, :hids], 0, 0).astype(bf)
    down_sums = lax.psum_scatter(grad_down, "dp", scatter_dimension=0, tiled=True)
    down_sums = lax.optimization_barrier(down_sums)

    def next_half(pending, step, *others):
        if not halving or step == ring:
            return pending, step
        keep, got = pending
        if others:
            got = after(got, *others)
        total = (keep.astype(fl) + got.astype(fl)).astype(bf)
        step *= 2
        if step == ring:
            return total, step
        return exchange_half(total, "dp", step), step

    d_h1, d_h1_b, d_qkv = [], [], ()
    g2, c2, bo = 0.0, 0.0, 0.0
    for i in range(images):
        at = slice(i * size, (i + 1) * size)
        got = after(received[i], grad_down, *d_qkv)
        total = dxn_parts[i].astype(fl)
        for other in got:
            total = total + other.astype(fl)
        back, hat = normalize_back(h1[at], ln_gain[1], total)
        g2 = g2 + jnp.sum(total * hat, axis=0)
        c2 = c2 + jnp.sum(total, axis=0)
        full = dy_all[at].astype(fl) + back
        bo = bo + jnp.sum(full, axis=0)
        d_h1.append(full)
        d_h1_b.append(full.astype(bf))
        d_att = dot(d_h1_b[i], own_out, 1, 0).astype(bf)
        d_qkv = (
            attention_backward(qkv, key_bias, attended[i], d_att, lses[i], d_qkv, i, size, heads),
        )
    (d_qkv,) = d_qkv

    y_all = after(jnp.stack(y_parts), got)
    h1_own = lax.dynamic_slice_in_dim(h1.reshape(images, size, width), where * rowp, rowp, 1)
    y_own = h1_own + sum_of(send_blocks(y_all, where, parts, rowp)) + out_bias[1]
    output = jnp.where(own_valid, y_own, 0.0).astype(bf)

    grad_qkv = dot(xn1, d_qkv, 0, 0).astype(bf)
    grad_out = dot(jnp.concatenate(d_h1_b, axis=0), attended_all, 0, 0).astype(bf)
    att_grads = jnp.concatenate([grad_qkv, grad_out], axis=1)
    att_sums = lax.psum_scatter(att_grads, "dp", scatter_dimension=0, tiled=True)

    d_qkv = after(d_qkv, att_grads)
    sums_qkv = jnp.sum(d_qkv.astype(fl), axis=0)
    d_xn1 = dot(d_qkv, full_qkv, 1, 1).astype(bf).reshape(images, size, width)
    shares = send_blocks(d_xn1, where, parts, rowp)
    d_pre = after(d_pre, d_xn1)
    grad_up = dot(xn2, d_pre[:, :hids], 0, 0).astype(bf)
    if halving:
        up_sums, step = grad_up.reshape(ring, here, hids), 1
        pending = exchange_half(up_sums, "dp", step)
    else:
        up_sums, step, pending = lax.psum_scatter(grad_up, "dp", tiled=True), ring, ()
    pending, step = next_half(pending, step)
    if halving:
        shares = after(shares, *pending[:1])
    d_xn1 = sum_of(shares)
    back, hat = normalize_back(x_own.astype(fl), ln_gain[0], d_xn1)
    g1 = jnp.sum(d_xn1 * hat, axis=(0, 1))
    c1 = jnp.sum(d_xn1, axis=(0, 1))
    pending, step = next_half(pending, step, g1)
    d_h1_own = jnp.stack([lax.dynamic_slice_in_dim(d, where * rowp, rowp, 0) for d in d_h1])
    d_inputs = (d_h1_own + back).astype(bf)

    b2 = jnp.sum(dy_own.astype(fl), axis=(0, 1))
    pair = jnp.stack([g1, g2 / parts, c1, c2 / parts, bo / parts, b2])
    pair = sum_everywhere(pair, "tensor")
    lone = jnp.concatenate([sums_qkv[:cols], sums_qkv[2 * colp : 2 * colp + cols], grad_b1[:hidden]])
    small = sum_everywhere(jnp.concatenate([pair.reshape(-1), lone]), "dp")
    pair = small[: 6 * width].reshape(6, width)
    lone = small[6 * width :]

    while halving and step < ring:
        pending, step = next_half(pending, step)
    if halving:
        up_sums = pending[0]

    def own_rows(values):
        return jnp.transpose(values[:, :rows], (1, 0, 2))

    return (
        own_rows(output),
        own_rows(d_inputs),
        pair[0:2],
        pair[2:4],
        att_sums[:, : 3 * colp].reshape(here, 3, colp)[:, :, :cols].astype(fl),
        lone[: 2 * cols].reshape(2, cols),
        transposed(att_sums[:, 3 * colp : 3 * colp + cols]),
        pair[4:6],
        up_sums[:, :hidden].astype(fl),
        lone[2 * cols :],
        transposed(down_sums)[:hidden],
    )


def solution(mesh):
    return jax.shard_map(
        on_device,
        mesh=mesh,
        in_specs=(
            P("tensor", "dp", None),
            P("dp"),
            P("tensor", "dp", None),
            P(),
            P(),
            P("dp", None, "tensor"),
            P(None, "tensor"),
            P("tensor", "dp"),
            P(),
            P("dp", "tensor"),
            P("tensor"),
            P("tensor", "dp"),
        ),
        out_specs=(
            P("tensor", "dp", None),
            P("tensor", "dp", None),
            P(),
            P(),
            P("dp", None, "tensor"),
            P(None, "tensor"),
            P("tensor", "dp"),
            P(),
            P("dp", "tensor"),
            P("tensor"),
            P("tensor", "dp"),
        ),
        check_vma=False,
    )
```

```python
import functools

import jax
import jax.numpy as jnp
from jax import lax
from jax.experimental import pallas as pl
from jax.experimental.pallas import tpu as pltpu
from jax.sharding import PartitionSpec as P


HD = 72
epsilon = 1e-06
fl = jnp.float32
bf = jnp.bfloat16


def up_to(n, m):
    return -(-n // m) * m


def dot(a, b, ca, cb):
    return lax.dot_general(a, b, (((ca,), (cb,)), ((), ())), preferred_element_type=fl)


def moments(values):
    mean = jnp.mean(values, axis=-1, keepdims=True)
    centred = values - mean
    variance = jnp.mean(centred * centred, axis=-1, keepdims=True)
    return mean, lax.rsqrt(variance + epsilon)


def normalize(values, mean, inverse, gain, shift):
    return (values - mean) * inverse * gain + shift


def normalize_back(values, mean, inverse, gain, grad):
    hat = (values - mean) * inverse
    scaled = grad * gain
    first = jnp.mean(scaled, axis=-1, keepdims=True)
    second = jnp.mean(scaled * hat, axis=-1, keepdims=True)
    return inverse * (scaled - first - hat * second), hat


def window(head, colp, win):
    start = jnp.minimum(head * HD // 128 * 128, colp - win)
    return pl.multiple_of(start, 128), head * HD - start


def forward_kernel(bias_ref, qkv_ref, out_ref, lse_ref, *, heads, colp, win):
    scale = HD ** (-0.5)
    out_ref[...] = jnp.zeros_like(out_ref)

    def one_head(head, carry):
        at, off = window(head, colp, win)
        lane = lax.broadcasted_iota(jnp.int32, (1, win), 1)
        mine = (lane >= off) & (lane < off + HD)
        query = qkv_ref[:, pl.ds(at, win)]
        keys = qkv_ref[:, pl.ds(pl.multiple_of(colp + at, 128), win)]
        values = qkv_ref[:, pl.ds(pl.multiple_of(2 * colp + at, 128), win)]
        keys = jnp.where(mine, keys, jnp.zeros_like(keys))
        values = jnp.where(mine, values, jnp.zeros_like(values))
        raw = dot(keys, query, 1, 1) * scale + bias_ref[...]
        top = jnp.max(raw, axis=0, keepdims=True)
        weights = jnp.exp(raw - top)
        total = jnp.sum(weights, axis=0, keepdims=True)
        result = dot(values, weights.astype(bf), 0, 0) / total
        lse_ref[pl.ds(head, 1), :] = top + jnp.log(total)
        out_ref[:, pl.ds(at, win)] = out_ref[:, pl.ds(at, win)] + result.T.astype(bf)
        return carry

    lax.fori_loop(0, heads, one_head, 0)


def attention_forward(qkv, bias, image, size, heads):
    colp = qkv.shape[1] // 3
    win = min(256, colp)
    return pl.pallas_call(
        functools.partial(forward_kernel, heads=heads, colp=colp, win=win),
        grid=(1,),
        out_shape=(
            jax.ShapeDtypeStruct((size, colp), bf),
            jax.ShapeDtypeStruct((heads, size), fl),
        ),
        in_specs=[
            pl.BlockSpec((size, 1), lambda g: (image, 0)),
            pl.BlockSpec((size, 3 * colp), lambda g: (image, 0)),
        ],
        out_specs=(
            pl.BlockSpec((size, colp), lambda g: (0, 0)),
            pl.BlockSpec((heads, size), lambda g: (0, 0)),
        ),
        compiler_params=pltpu.CompilerParams(vmem_limit_bytes=56 * 2**20),
        cost_estimate=pl.CostEstimate(
            flops=4 * heads * size * size * win,
            bytes_accessed=8 * size * colp,
            transcendentals=heads * size * size,
        ),
        name="attention_forward",
    )(bias, qkv)


def backward_kernel(
    bias_ref, qkv_ref, out_ref, dout_ref, lse_ref, *refs, heads, colp, win
):
    dqkv_ref = refs[-1]
    scale = HD ** (-0.5)
    dqkv_ref[...] = jnp.zeros_like(dqkv_ref)

    def one_head(head, carry):
        at, off = window(head, colp, win)
        at_k = pl.multiple_of(colp + at, 128)
        at_v = pl.multiple_of(2 * colp + at, 128)
        lane = lax.broadcasted_iota(jnp.int32, (1, win), 1)
        mine = (lane >= off) & (lane < off + HD)

        def keep(block):
            return jnp.where(mine, block, jnp.zeros_like(block))

        query = keep(qkv_ref[:, pl.ds(at, win)])
        keys = keep(qkv_ref[:, pl.ds(at_k, win)])
        values = keep(qkv_ref[:, pl.ds(at_v, win)])
        d_out = keep(dout_ref[:, pl.ds(at, win)])
        product = d_out.astype(fl) * out_ref[:, pl.ds(at, win)].astype(fl)
        delta = jnp.sum(product, axis=1, keepdims=True).T
        raw = dot(keys, query, 1, 1) * scale + bias_ref[...]
        probs = jnp.exp(raw - lse_ref[pl.ds(head, 1), :])
        d_probs = dot(values, d_out, 1, 1)
        d_raw = (probs * ((d_probs - delta) * scale)).astype(bf)

        def add(place, block):
            dqkv_ref[:, pl.ds(place, win)] = dqkv_ref[:, pl.ds(place, win)] + block.astype(bf)

        add(at_v, dot(probs.astype(bf), d_out, 1, 0))
        add(at_k, dot(d_raw, query, 1, 0))
        add(at, dot(keys, d_raw, 0, 0).T)
        return carry

    lax.fori_loop(0, heads, one_head, 0)


def attention_backward(qkv, bias, attended, d_attended, lse, old, image, size, heads):
    colp = qkv.shape[1] // 3
    win = min(256, colp)
    return pl.pallas_call(
        functools.partial(backward_kernel, heads=heads, colp=colp, win=win),
        grid=(1,),
        out_shape=jax.ShapeDtypeStruct(qkv.shape, bf),
        in_specs=[
            pl.BlockSpec((size, 1), lambda g: (image, 0)),
            pl.BlockSpec((size, 3 * colp), lambda g: (image, 0)),
            pl.BlockSpec((size, colp), lambda g: (0, 0)),
            pl.BlockSpec((size, colp), lambda g: (0, 0)),
            pl.BlockSpec((heads, size), lambda g: (0, 0)),
        ]
        + [pl.BlockSpec(memory_space=pl.ANY)] * len(old),
        out_specs=pl.BlockSpec((size, 3 * colp), lambda g: (image, 0)),
        input_output_aliases={5 + k: k for k in range(len(old))},
        compiler_params=pltpu.CompilerParams(vmem_limit_bytes=56 * 2**20),
        cost_estimate=pl.CostEstimate(
            flops=10 * heads * size * size * win,
            bytes_accessed=16 * size * colp,
            transcendentals=heads * size * size,
        ),
        name="attention_backward",
    )(bias, qkv, attended, d_attended, lse, *old)


def mlp_kernel(xn_ref, dy_ref, up_ref, down_ref, bias_ref, *refs):
    act_ref, dpre_ref, sum_ref, y_ref, dxn_ref, y_acc, dxn_acc = refs[-7:]
    step = pl.program_id(0)
    root = (2.0 / jnp.pi) ** 0.5

    @pl.when(step == 0)
    def _():
        y_acc[...] = jnp.zeros_like(y_acc)
        dxn_acc[...] = jnp.zeros_like(dxn_acc)

    up, down = up_ref[...], down_ref[...]
    pre = dot(xn_ref[...], up, 1, 0) + bias_ref[...]
    d_act = dot(dy_ref[...], down, 1, 0)
    square = pre * pre
    tanh = jnp.tanh(pre * (root + root * 0.044715 * square))
    half = 0.5 + 0.5 * tanh
    slope = half + (pre * (0.5 - 0.5 * tanh * tanh)) * (root + 3.0 * root * 0.044715 * square)
    d_pre = d_act * slope
    sum_ref[...] = jnp.sum(d_pre, axis=0, keepdims=True)
    act = (pre * half).astype(bf)
    d_pre = d_pre.astype(bf)
    act_ref[...] = act
    dpre_ref[...] = d_pre
    y_acc[...] += dot(act, down, 1, 1)
    dxn_acc[...] += dot(d_pre, up, 1, 1)

    @pl.when(step == pl.num_programs(0) - 1)
    def _():
        y_ref[...] = y_acc[...].astype(bf)
        dxn_ref[...] = dxn_acc[...].astype(bf)


def mlp(xn, dy, weights, bias, old, image, size, tile):
    both, width = xn.shape
    hidp = bias.shape[1]
    steps = hidp // tile
    rows = pl.BlockSpec((size, width), lambda g: (image, 0))
    wide = pl.BlockSpec((size, tile), lambda g: (image, g))
    whole = pl.BlockSpec((size, width), lambda g: (0, 0))
    return pl.pallas_call(
        mlp_kernel,
        grid=(steps,),
        out_shape=(
            jax.ShapeDtypeStruct((both, hidp), bf),
            jax.ShapeDtypeStruct((both, hidp), bf),
            jax.ShapeDtypeStruct((1, hidp), fl),
            jax.ShapeDtypeStruct((size, width), bf),
            jax.ShapeDtypeStruct((size, width), bf),
        ),
        in_specs=[
            rows,
            rows,
            pl.BlockSpec((width, tile), lambda g: (0, g)),
            pl.BlockSpec((width, tile), lambda g: (0, steps + g)),
            pl.BlockSpec((1, tile), lambda g: (0, g)),
        ]
        + [pl.BlockSpec(memory_space=pl.ANY)] * len(old),
        out_specs=(wide, wide, pl.BlockSpec((1, tile), lambda g: (0, g)), whole, whole),
        scratch_shapes=[pltpu.VMEM((size, width), fl)] * 2,
        input_output_aliases={5 + k: k for k in range(len(old))},
        compiler_params=pltpu.CompilerParams(vmem_limit_bytes=56 * 2**20),
        cost_estimate=pl.CostEstimate(
            flops=8 * size * width * hidp,
            bytes_accessed=4 * width * (hidp + 2 * size) + 4 * size * hidp,
            transcendentals=size * hidp,
        ),
        name="mlp",
    )(xn, dy, weights, weights, bias, *old)


def from_others(values, parts):
    return [
        lax.ppermute(values, "tensor", [((j + k) % parts, j) for j in range(parts)])
        for k in range(1, parts)
    ]


def all_blocks(values, got, where):
    images, rows, width = values.shape
    got = [values] + got
    parts = len(got)
    full = jnp.zeros((images, rows * parts, width), values.dtype)
    for k, block in enumerate(got):
        start = (where + k) % parts * rows
        full = lax.dynamic_update_slice(full, block, (jnp.int32(0), start, jnp.int32(0)))
    return full


def send_blocks(values, where, parts, rows):
    def block(k):
        start = (where + k) % parts * rows
        return jnp.stack([lax.dynamic_slice_in_dim(v, start, rows, 0) for v in values])

    shares = [block(0)]
    for k in range(1, parts):
        pairs = [(j, (j + k) % parts) for j in range(parts)]
        shares.append(lax.ppermute(block(k), "tensor", pairs))
    return shares


def sum_of(shares):
    return functools.reduce(jnp.add, [share.astype(fl) for share in shares])


def start_doubling(have, axis, step):
    size = lax.axis_size(axis)
    return have, lax.ppermute(have, axis, [(j, j ^ step) for j in range(size)])


def end_doubling(have, got, axis, step):
    first = lax.axis_index(axis) // step % 2 == 0
    low, high = jnp.where(first, have, got), jnp.where(first, got, have)
    return jnp.stack([low, high], axis=1).reshape(-1, *have.shape[1:])


def exchange_half(values, axis, step):
    size = lax.axis_size(axis)
    blocks, rows, width = values.shape
    split = values.reshape(blocks // 2, 2, rows, width)
    mine = lax.axis_index(axis) // step % 2
    send = lax.dynamic_index_in_dim(split, 1 - mine, 1, False)
    keep = lax.dynamic_index_in_dim(split, mine, 1, False)
    return keep, lax.ppermute(send, axis, [(j, j ^ step) for j in range(size)])


def sum_everywhere(values, axis):
    size = lax.axis_size(axis)
    if size & (size - 1):
        return lax.psum(values, axis)
    step = 1
    while step < size:
        values = values + lax.ppermute(values, axis, [(j, j ^ step) for j in range(size)])
        step *= 2
    return values


def after(values, *others):
    return lax.optimization_barrier((values, others))[0]


def transposed(values):
    return dot(values, jnp.eye(values.shape[0], dtype=values.dtype), 0, 0)


def on_device(
    inputs,
    lengths,
    cotangent,
    ln_gain,
    ln_bias,
    w_qkv,
    qv_bias,
    w_out,
    out_bias,
    w_up,
    up_bias,
    w_down,
):
    rows, images, width = inputs.shape
    parts = lax.axis_size("tensor")
    where = lax.axis_index("tensor")
    cols = w_qkv.shape[2]
    hidden = up_bias.shape[0]
    heads = cols // HD
    here = w_qkv.shape[0]
    rowp, colp, hids, hidp = up_to(rows, 16), up_to(cols, 128), up_to(hidden, 128), up_to(hidden, 256)
    tile = next(256 * k for k in (3, 2, 1) if hidp % (256 * k) == 0)
    size = rowp * parts
    both = images * size

    def pad_to(values, axis, n):
        widths = [(0, 0)] * values.ndim
        widths[axis] = (0, n - values.shape[axis])
        return jnp.pad(values, widths)

    x_own = pad_to(jnp.transpose(inputs, (1, 0, 2)), 1, rowp)
    x_all = all_blocks(x_own, from_others(x_own, parts), where).reshape(both, width)

    shard_qkv = pad_to(w_qkv, 2, colp).reshape(here, 3 * colp)
    full_qkv = lax.all_gather(shard_qkv, "dp", axis=0, tiled=True)
    shard_out = pad_to(w_out.T, 1, colp)
    shard_out = jnp.concatenate([shard_out] + from_others(shard_out, parts), axis=1)
    ring = lax.axis_size("dp")
    halving = not ring & (ring - 1)
    shard_mlp = jnp.concatenate([pad_to(w_up, 1, hidp), pad_to(w_down.T, 1, hidp)], axis=1)
    full_mlp = lax.all_gather(shard_mlp, "dp", axis=0, tiled=True)

    place = jnp.arange(size, dtype=jnp.int32)
    position = place // rowp * rows + place % rowp
    valid = (place % rowp < rows)[None, :] & (position[None, :] < lengths[:, None])
    key_bias = jnp.where(valid, 0.0, -1e30).astype(fl).reshape(both, 1)
    own_valid = lax.dynamic_slice_in_dim(valid, where * rowp, rowp, 1)[:, :, None]

    dy_own = pad_to(jnp.transpose(cotangent, (1, 0, 2)), 1, rowp) * own_valid.astype(bf)
    dy_others = from_others(dy_own, parts)

    mean1, inverse1 = lax.optimization_barrier(moments(x_all.astype(fl)))
    xn1 = normalize(x_all.astype(fl), mean1, inverse1, ln_gain[0], ln_bias[0]).astype(bf)
    bias_three = pad_to(
        jnp.stack([qv_bias[0], jnp.zeros_like(qv_bias[0]), qv_bias[1]]), 1, colp
    ).reshape(1, 3 * colp)
    doubling = ring // 2
    if halving:
        pending = start_doubling(after(shard_out, full_qkv)[None], "dp", doubling)
    qkv = (dot(xn1, full_qkv, 1, 0) + bias_three).astype(bf)

    def next_double(pending, step, *others):
        if not halving or not step:
            return pending, step
        have, got = pending
        if others:
            got = after(got, *others)
        have = end_doubling(have, got, "dp", step)
        step //= 2
        return (start_doubling(have, "dp", step) if step else (have,)), step

    if halving:
        pending, doubling = next_double(pending, doubling, qkv)
    attended, lses, joined = [], [], []
    for i in range(images):
        out, lse = attention_forward(qkv, key_bias, i, size, heads)
        attended.append(out)
        lses.append(lse)
    if halving:
        pending, doubling = next_double(pending, doubling, *attended)
    attended = after(attended, *attended)
    for i in range(images):
        others = from_others(attended[i], parts)
        joined.append(jnp.concatenate([attended[i]] + others, axis=1))
    if halving:
        while doubling:
            pending, doubling = next_double(pending, doubling)
        full_out = pending[0].reshape(width, -1)
    else:
        full_out = lax.all_gather(shard_out, "dp", axis=0, tiled=True)
    own_out = full_out[:, :colp]
    dy_others = after(dy_others, *attended)
    dy_all = all_blocks(dy_own, dy_others, where).reshape(both, width)
    joined = jnp.concatenate(joined, axis=0)
    attended_all = joined[:, :colp]

    h1 = x_all.astype(fl) + dot(joined, full_out, 1, 1) + out_bias[0]
    mean2, inverse2 = lax.optimization_barrier(moments(h1))
    xn2 = normalize(h1, mean2, inverse2, ln_gain[1], ln_bias[1]).astype(bf)
    bias_up = pad_to(up_bias, 0, hidp)[None]
    wide, y_parts, dxn_parts, received, grad_b1 = (), [], [], [], 0.0
    for i in range(images):
        act, d_pre, sums, y_part, dxn = mlp(
            xn2, dy_all, full_mlp, bias_up, wide, i, size, tile
        )
        wide = (act, d_pre)
        grad_b1 = grad_b1 + sums[0]
        y_parts.append(y_part)
        dxn_parts.append(dxn)
        received.append(from_others(dxn, parts))
    grad_down = dot(dy_all, act[:, :hids], 0, 0).astype(bf)
    down_sums = lax.psum_scatter(grad_down, "dp", scatter_dimension=0, tiled=True)
    down_sums = lax.optimization_barrier(down_sums)

    def next_half(pending, step, *others):
        if not halving or step == ring:
            return pending, step
        keep, got = pending
        if others:
            got = after(got, *others)
        total = (keep.astype(fl) + got.astype(fl)).astype(bf)
        step *= 2
        if step == ring:
            return total, step
        return exchange_half(total, "dp", step), step

    d_h1, d_h1_b, d_qkv = [], [], ()
    g2, c2, bo = 0.0, 0.0, 0.0
    for i in range(images):
        at = slice(i * size, (i + 1) * size)
        got = after(received[i], grad_down, *d_qkv)
        total = dxn_parts[i].astype(fl)
        for other in got:
            total = total + other.astype(fl)
        back, hat = normalize_back(h1[at], mean2[at], inverse2[at], ln_gain[1], total)
        g2 = g2 + jnp.sum(total * hat, axis=0)
        c2 = c2 + jnp.sum(total, axis=0)
        full = dy_all[at].astype(fl) + back
        bo = bo + jnp.sum(full, axis=0)
        d_h1.append(full)
        d_h1_b.append(full.astype(bf))
        d_att = dot(d_h1_b[i], own_out, 1, 0).astype(bf)
        d_qkv = (
            attention_backward(qkv, key_bias, attended[i], d_att, lses[i], d_qkv, i, size, heads),
        )
    (d_qkv,) = d_qkv

    y_parts = after(y_parts, got)
    h1_own = lax.dynamic_slice_in_dim(h1.reshape(images, size, width), where * rowp, rowp, 1)
    y_own = h1_own + sum_of(send_blocks(y_parts, where, parts, rowp)) + out_bias[1]
    output = jnp.where(own_valid, y_own, 0.0).astype(bf)

    grad_qkv = dot(xn1, d_qkv, 0, 0).astype(bf)
    grad_out = dot(jnp.concatenate(d_h1_b, axis=0), attended_all, 0, 0).astype(bf)
    att_grads = jnp.concatenate([grad_qkv, grad_out], axis=1)
    att_sums = lax.psum_scatter(att_grads, "dp", scatter_dimension=0, tiled=True)

    d_pre = after(d_pre, att_grads)
    grad_up = dot(xn2, d_pre[:, :hids], 0, 0).astype(bf)
    if halving:
        up_sums, step = grad_up.reshape(ring, here, hids), 1
        pending = exchange_half(up_sums, "dp", step)
    else:
        up_sums, step, pending = lax.psum_scatter(grad_up, "dp", tiled=True), ring, ()
    d_qkv = after(d_qkv, grad_up)
    sums_qkv = jnp.sum(d_qkv.astype(fl), axis=0)
    d_xn1 = dot(d_qkv, full_qkv, 1, 1).astype(bf).reshape(images, size, width)
    d_xn1 = [d_xn1[i] for i in range(images)]
    shares = send_blocks(d_xn1, where, parts, rowp)
    pending, step = next_half(pending, step, d_xn1)
    if halving:
        shares = after(shares, *pending[:1])
    d_xn1 = sum_of(shares)

    def own_part(values):
        return lax.dynamic_slice_in_dim(values.reshape(images, size, 1), where * rowp, rowp, 1)

    back, hat = normalize_back(
        x_own.astype(fl), own_part(mean1), own_part(inverse1), ln_gain[0], d_xn1
    )
    g1 = jnp.sum(d_xn1 * hat, axis=(0, 1))
    c1 = jnp.sum(d_xn1, axis=(0, 1))
    pending, step = next_half(pending, step, g1)
    d_h1_own = jnp.stack([lax.dynamic_slice_in_dim(d, where * rowp, rowp, 0) for d in d_h1])
    d_inputs = (d_h1_own + back).astype(bf)

    b2 = jnp.sum(dy_own.astype(fl), axis=(0, 1))
    pair = jnp.stack([g1, g2 / parts, c1, c2 / parts, bo / parts, b2])
    pair = sum_everywhere(pair, "tensor")
    lone = jnp.concatenate([sums_qkv[:cols], sums_qkv[2 * colp : 2 * colp + cols], grad_b1[:hidden]])
    small = sum_everywhere(jnp.concatenate([pair.reshape(-1), lone]), "dp")
    pair = small[: 6 * width].reshape(6, width)
    lone = small[6 * width :]

    while halving and step < ring:
        pending, step = next_half(pending, step)
    if halving:
        up_sums = pending[0]

    def own_rows(values):
        return jnp.transpose(values[:, :rows], (1, 0, 2))

    return (
        own_rows(output),
        own_rows(d_inputs),
        pair[0:2],
        pair[2:4],
        att_sums[:, : 3 * colp].reshape(here, 3, colp)[:, :, :cols].astype(fl),
        lone[: 2 * cols].reshape(2, cols),
        transposed(att_sums[:, 3 * colp : 3 * colp + cols]),
        pair[4:6],
        up_sums[:, :hidden].astype(fl),
        lone[2 * cols :],
        transposed(down_sums)[:hidden],
    )


def solution(mesh):
    return jax.shard_map(
        on_device,
        mesh=mesh,
        in_specs=(
            P("tensor", "dp", None),
            P("dp"),
            P("tensor", "dp", None),
            P(),
            P(),
            P("dp", None, "tensor"),
            P(None, "tensor"),
            P("tensor", "dp"),
            P(),
            P("dp", "tensor"),
            P("tensor"),
            P("tensor", "dp"),
        ),
        out_specs=(
            P("tensor", "dp", None),
            P("tensor", "dp", None),
            P(),
            P(),
            P("dp", None, "tensor"),
            P(None, "tensor"),
            P("tensor", "dp"),
            P(),
            P("dp", "tensor"),
            P("tensor"),
            P("tensor", "dp"),
        ),
        check_vma=False,
    )
```

```python
import functools

import jax
import jax.numpy as jnp
from jax import lax
from jax.experimental import pallas as pl
from jax.experimental.pallas import tpu as pltpu
from jax.sharding import PartitionSpec as P


HD = 72
epsilon = 1e-06
fl = jnp.float32
bf = jnp.bfloat16


def up_to(n, m):
    return -(-n // m) * m


def dot(a, b, ca, cb):
    return lax.dot_general(a, b, (((ca,), (cb,)), ((), ())), preferred_element_type=fl)


def moments(values):
    mean = jnp.mean(values, axis=-1, keepdims=True)
    centred = values - mean
    variance = jnp.mean(centred * centred, axis=-1, keepdims=True)
    return mean, lax.rsqrt(variance + epsilon)


def normalize(values, mean, inverse, gain, shift):
    return (values - mean) * inverse * gain + shift


def normalize_back(values, mean, inverse, gain, grad):
    hat = (values - mean) * inverse
    scaled = grad * gain
    first = jnp.mean(scaled, axis=-1, keepdims=True)
    second = jnp.mean(scaled * hat, axis=-1, keepdims=True)
    return inverse * (scaled - first - hat * second), hat


def window(head, colp, win):
    start = jnp.minimum(head * HD // 128 * 128, colp - win)
    return pl.multiple_of(start, 128), head * HD - start


def forward_kernel(bias_ref, qkv_ref, out_ref, lse_ref, *, heads, colp, win):
    scale = HD ** (-0.5)
    out_ref[...] = jnp.zeros_like(out_ref)

    def one_head(head, carry):
        at, off = window(head, colp, win)
        lane = lax.broadcasted_iota(jnp.int32, (1, win), 1)
        mine = (lane >= off) & (lane < off + HD)
        query = qkv_ref[:, pl.ds(at, win)]
        keys = qkv_ref[:, pl.ds(pl.multiple_of(colp + at, 128), win)]
        values = qkv_ref[:, pl.ds(pl.multiple_of(2 * colp + at, 128), win)]
        keys = jnp.where(mine, keys, jnp.zeros_like(keys))
        values = jnp.where(mine, values, jnp.zeros_like(values))
        raw = dot(keys, query, 1, 1) * scale + bias_ref[...]
        top = jnp.max(raw, axis=0, keepdims=True)
        weights = jnp.exp(raw - top)
        total = jnp.sum(weights, axis=0, keepdims=True)
        result = dot(values, weights.astype(bf), 0, 0) / total
        lse_ref[pl.ds(head, 1), :] = top + jnp.log(total)
        out_ref[:, pl.ds(at, win)] = out_ref[:, pl.ds(at, win)] + result.T.astype(bf)
        return carry

    lax.fori_loop(0, heads, one_head, 0)


def attention_forward(qkv, bias, image, size, heads):
    colp = qkv.shape[1] // 3
    win = min(256, colp)
    return pl.pallas_call(
        functools.partial(forward_kernel, heads=heads, colp=colp, win=win),
        grid=(1,),
        out_shape=(
            jax.ShapeDtypeStruct((size, colp), bf),
            jax.ShapeDtypeStruct((heads, size), fl),
        ),
        in_specs=[
            pl.BlockSpec((size, 1), lambda g: (image, 0)),
            pl.BlockSpec((size, 3 * colp), lambda g: (image, 0)),
        ],
        out_specs=(
            pl.BlockSpec((size, colp), lambda g: (0, 0)),
            pl.BlockSpec((heads, size), lambda g: (0, 0)),
        ),
        compiler_params=pltpu.CompilerParams(vmem_limit_bytes=56 * 2**20),
        cost_estimate=pl.CostEstimate(
            flops=4 * heads * size * size * win,
            bytes_accessed=8 * size * colp,
            transcendentals=heads * size * size,
        ),
        name="attention_forward",
    )(bias, qkv)


def backward_kernel(
    bias_ref, qkv_ref, out_ref, dout_ref, lse_ref, *refs, heads, colp, win
):
    dqkv_ref = refs[-1]
    scale = HD ** (-0.5)
    dqkv_ref[...] = jnp.zeros_like(dqkv_ref)

    def one_head(head, carry):
        at, off = window(head, colp, win)
        at_k = pl.multiple_of(colp + at, 128)
        at_v = pl.multiple_of(2 * colp + at, 128)
        lane = lax.broadcasted_iota(jnp.int32, (1, win), 1)
        mine = (lane >= off) & (lane < off + HD)

        def keep(block):
            return jnp.where(mine, block, jnp.zeros_like(block))

        query = keep(qkv_ref[:, pl.ds(at, win)])
        keys = keep(qkv_ref[:, pl.ds(at_k, win)])
        values = keep(qkv_ref[:, pl.ds(at_v, win)])
        d_out = keep(dout_ref[:, pl.ds(at, win)])
        product = d_out.astype(fl) * out_ref[:, pl.ds(at, win)].astype(fl)
        delta = jnp.sum(product, axis=1, keepdims=True).T
        raw = dot(keys, query, 1, 1) * scale + bias_ref[...]
        probs = jnp.exp(raw - lse_ref[pl.ds(head, 1), :])
        d_probs = dot(values, d_out, 1, 1)
        d_raw = (probs * ((d_probs - delta) * scale)).astype(bf)

        def add(place, block):
            dqkv_ref[:, pl.ds(place, win)] = dqkv_ref[:, pl.ds(place, win)] + block.astype(bf)

        add(at_v, dot(probs.astype(bf), d_out, 1, 0))
        add(at_k, dot(d_raw, query, 1, 0))
        add(at, dot(keys, d_raw, 0, 0).T)
        return carry

    lax.fori_loop(0, heads, one_head, 0)


def attention_backward(qkv, bias, attended, d_attended, lse, old, image, size, heads):
    colp = qkv.shape[1] // 3
    win = min(256, colp)
    return pl.pallas_call(
        functools.partial(backward_kernel, heads=heads, colp=colp, win=win),
        grid=(1,),
        out_shape=jax.ShapeDtypeStruct(qkv.shape, bf),
        in_specs=[
            pl.BlockSpec((size, 1), lambda g: (image, 0)),
            pl.BlockSpec((size, 3 * colp), lambda g: (image, 0)),
            pl.BlockSpec((size, colp), lambda g: (0, 0)),
            pl.BlockSpec((size, colp), lambda g: (0, 0)),
            pl.BlockSpec((heads, size), lambda g: (0, 0)),
        ]
        + [pl.BlockSpec(memory_space=pl.ANY)] * len(old),
        out_specs=pl.BlockSpec((size, 3 * colp), lambda g: (image, 0)),
        input_output_aliases={5 + k: k for k in range(len(old))},
        compiler_params=pltpu.CompilerParams(vmem_limit_bytes=56 * 2**20),
        cost_estimate=pl.CostEstimate(
            flops=10 * heads * size * size * win,
            bytes_accessed=16 * size * colp,
            transcendentals=heads * size * size,
        ),
        name="attention_backward",
    )(bias, qkv, attended, d_attended, lse, *old)


def mlp_kernel(xn_ref, dy_ref, up_ref, down_ref, bias_ref, *refs):
    act_ref, dpre_ref, sum_ref, y_ref, dxn_ref, y_acc, dxn_acc = refs[-7:]
    step = pl.program_id(0)
    root = (2.0 / jnp.pi) ** 0.5

    @pl.when(step == 0)
    def _():
        y_acc[...] = jnp.zeros_like(y_acc)
        dxn_acc[...] = jnp.zeros_like(dxn_acc)

    up, down = up_ref[...], down_ref[...]
    pre = dot(xn_ref[...], up, 1, 0) + bias_ref[...]
    d_act = dot(dy_ref[...], down, 1, 0)
    square = pre * pre
    tanh = jnp.tanh(pre * (root + root * 0.044715 * square))
    half = 0.5 + 0.5 * tanh
    slope = half + (pre * (0.5 - 0.5 * tanh * tanh)) * (root + 3.0 * root * 0.044715 * square)
    d_pre = d_act * slope
    sum_ref[...] = jnp.sum(d_pre, axis=0, keepdims=True)
    act = (pre * half).astype(bf)
    d_pre = d_pre.astype(bf)
    act_ref[...] = act
    dpre_ref[...] = d_pre
    y_acc[...] += dot(act, down, 1, 1)
    dxn_acc[...] += dot(d_pre, up, 1, 1)

    @pl.when(step == pl.num_programs(0) - 1)
    def _():
        y_ref[...] = y_acc[...].astype(bf)
        dxn_ref[...] = dxn_acc[...].astype(bf)


def mlp(xn, dy, weights, bias, old, image, size, tile):
    both, width = xn.shape
    hidp = bias.shape[1]
    steps = hidp // tile
    rows = pl.BlockSpec((size, width), lambda g: (image, 0))
    wide = pl.BlockSpec((size, tile), lambda g: (image, g))
    whole = pl.BlockSpec((size, width), lambda g: (0, 0))
    return pl.pallas_call(
        mlp_kernel,
        grid=(steps,),
        out_shape=(
            jax.ShapeDtypeStruct((both, hidp), bf),
            jax.ShapeDtypeStruct((both, hidp), bf),
            jax.ShapeDtypeStruct((1, hidp), fl),
            jax.ShapeDtypeStruct((size, width), bf),
            jax.ShapeDtypeStruct((size, width), bf),
        ),
        in_specs=[
            rows,
            rows,
            pl.BlockSpec((width, tile), lambda g: (0, g)),
            pl.BlockSpec((width, tile), lambda g: (0, steps + g)),
            pl.BlockSpec((1, tile), lambda g: (0, g)),
        ]
        + [pl.BlockSpec(memory_space=pl.ANY)] * len(old),
        out_specs=(wide, wide, pl.BlockSpec((1, tile), lambda g: (0, g)), whole, whole),
        scratch_shapes=[pltpu.VMEM((size, width), fl)] * 2,
        input_output_aliases={5 + k: k for k in range(len(old))},
        compiler_params=pltpu.CompilerParams(vmem_limit_bytes=56 * 2**20),
        cost_estimate=pl.CostEstimate(
            flops=8 * size * width * hidp,
            bytes_accessed=4 * width * (hidp + 2 * size) + 4 * size * hidp,
            transcendentals=size * hidp,
        ),
        name="mlp",
    )(xn, dy, weights, weights, bias, *old)


def from_others(values, parts):
    return [
        lax.ppermute(values, "tensor", [((j + k) % parts, j) for j in range(parts)])
        for k in range(1, parts)
    ]


def all_blocks(values, got, where):
    images, rows, width = values.shape
    got = [values] + got
    parts = len(got)
    full = jnp.zeros((images, rows * parts, width), values.dtype)
    for k, block in enumerate(got):
        start = (where + k) % parts * rows
        full = lax.dynamic_update_slice(full, block, (jnp.int32(0), start, jnp.int32(0)))
    return full


def send_blocks(values, where, parts, rows):
    def block(k):
        start = (where + k) % parts * rows
        return jnp.stack([lax.dynamic_slice_in_dim(v, start, rows, 0) for v in values])

    shares = [block(0)]
    for k in range(1, parts):
        pairs = [(j, (j + k) % parts) for j in range(parts)]
        shares.append(lax.ppermute(block(k), "tensor", pairs))
    return shares


def sum_of(shares):
    return functools.reduce(jnp.add, [share.astype(fl) for share in shares])


def start_doubling(have, axis, step):
    size = lax.axis_size(axis)
    return have, lax.ppermute(have, axis, [(j, j ^ step) for j in range(size)])


def end_doubling(have, got, axis, step):
    first = lax.axis_index(axis) // step % 2 == 0
    low, high = jnp.where(first, have, got), jnp.where(first, got, have)
    return jnp.stack([low, high], axis=1).reshape(-1, *have.shape[1:])


def exchange_half(values, axis, step):
    size = lax.axis_size(axis)
    blocks, rows, width = values.shape
    split = values.reshape(blocks // 2, 2, rows, width)
    mine = lax.axis_index(axis) // step % 2
    send = lax.dynamic_index_in_dim(split, 1 - mine, 1, False)
    keep = lax.dynamic_index_in_dim(split, mine, 1, False)
    return keep, lax.ppermute(send, axis, [(j, j ^ step) for j in range(size)])


def sum_everywhere(values, axis):
    size = lax.axis_size(axis)
    if size & (size - 1):
        return lax.psum(values, axis)
    step = 1
    while step < size:
        values = values + lax.ppermute(values, axis, [(j, j ^ step) for j in range(size)])
        step *= 2
    return values


def after(values, *others):
    return lax.optimization_barrier((values, others))[0]


def transposed(values):
    return dot(values, jnp.eye(values.shape[0], dtype=values.dtype), 0, 0)


def on_device(
    inputs,
    lengths,
    cotangent,
    ln_gain,
    ln_bias,
    w_qkv,
    qv_bias,
    w_out,
    out_bias,
    w_up,
    up_bias,
    w_down,
):
    rows, images, width = inputs.shape
    parts = lax.axis_size("tensor")
    where = lax.axis_index("tensor")
    cols = w_qkv.shape[2]
    hidden = up_bias.shape[0]
    heads = cols // HD
    here = w_qkv.shape[0]
    rowp, colp, hids, hidp = up_to(rows, 16), up_to(cols, 128), up_to(hidden, 128), up_to(hidden, 256)
    tile = next(256 * k for k in (3, 2, 1) if hidp % (256 * k) == 0)
    size = rowp * parts
    both = images * size

    def pad_to(values, axis, n):
        widths = [(0, 0)] * values.ndim
        widths[axis] = (0, n - values.shape[axis])
        return jnp.pad(values, widths)

    x_own = pad_to(jnp.transpose(inputs, (1, 0, 2)), 1, rowp)
    x_all = all_blocks(x_own, from_others(x_own, parts), where).reshape(both, width)

    shard_qkv = pad_to(w_qkv, 2, colp).reshape(here, 3 * colp)
    full_qkv = lax.all_gather(shard_qkv, "dp", axis=0, tiled=True)
    shard_out = pad_to(w_out.T, 1, colp)
    shard_out = jnp.concatenate([shard_out] + from_others(shard_out, parts), axis=1)
    ring = lax.axis_size("dp")
    halving = not ring & (ring - 1)
    shard_mlp = jnp.concatenate([pad_to(w_up, 1, hidp), pad_to(w_down.T, 1, hidp)], axis=1)
    full_mlp = lax.all_gather(shard_mlp, "dp", axis=0, tiled=True)

    place = jnp.arange(size, dtype=jnp.int32)
    position = place // rowp * rows + place % rowp
    valid = (place % rowp < rows)[None, :] & (position[None, :] < lengths[:, None])
    key_bias = jnp.where(valid, 0.0, -1e30).astype(fl).reshape(both, 1)
    own_valid = lax.dynamic_slice_in_dim(valid, where * rowp, rowp, 1)[:, :, None]

    dy_own = pad_to(jnp.transpose(cotangent, (1, 0, 2)), 1, rowp) * own_valid.astype(bf)
    dy_others = from_others(dy_own, parts)

    mean1, inverse1 = lax.optimization_barrier(moments(x_all.astype(fl)))
    xn1 = normalize(x_all.astype(fl), mean1, inverse1, ln_gain[0], ln_bias[0]).astype(bf)
    bias_three = pad_to(
        jnp.stack([qv_bias[0], jnp.zeros_like(qv_bias[0]), qv_bias[1]]), 1, colp
    ).reshape(1, 3 * colp)
    doubling = ring // 2
    if halving:
        pending = start_doubling(after(shard_out, full_qkv)[None], "dp", doubling)
    qkv = (dot(xn1, full_qkv, 1, 0) + bias_three).astype(bf)

    def next_double(pending, step, *others):
        if not halving or not step:
            return pending, step
        have, got = pending
        if others:
            got = after(got, *others)
        have = end_doubling(have, got, "dp", step)
        step //= 2
        return (start_doubling(have, "dp", step) if step else (have,)), step

    if halving:
        pending, doubling = next_double(pending, doubling, qkv)
    attended, lses, joined = [], [], []
    for i in range(images):
        out, lse = attention_forward(qkv, key_bias, i, size, heads)
        attended.append(out)
        lses.append(lse)
    if halving:
        pending, doubling = next_double(pending, doubling, *attended)
    attended = after(attended, *attended)
    for i in range(images):
        others = from_others(attended[i], parts)
        joined.append(jnp.concatenate([attended[i]] + others, axis=1))
    if halving:
        while doubling:
            pending, doubling = next_double(pending, doubling)
        full_out = pending[0].reshape(width, -1)
    else:
        full_out = lax.all_gather(shard_out, "dp", axis=0, tiled=True)
    own_out = full_out[:, :colp]
    dy_others = after(dy_others, *attended)
    dy_all = all_blocks(dy_own, dy_others, where).reshape(both, width)
    joined = jnp.concatenate(joined, axis=0)
    attended_all = joined[:, :colp]

    h1 = x_all.astype(fl) + dot(joined, full_out, 1, 1) + out_bias[0]
    mean2, inverse2 = lax.optimization_barrier(moments(h1))
    xn2 = normalize(h1, mean2, inverse2, ln_gain[1], ln_bias[1]).astype(bf)
    bias_up = pad_to(up_bias, 0, hidp)[None]
    wide, y_parts, dxn_parts, received, grad_b1 = (), [], [], [], 0.0
    for i in range(images):
        act, d_pre, sums, y_part, dxn = mlp(
            xn2, dy_all, full_mlp, bias_up, wide, i, size, tile
        )
        wide = (act, d_pre)
        grad_b1 = grad_b1 + sums[0]
        y_parts.append(y_part)
        dxn_parts.append(dxn)
        received.append(from_others(dxn, parts))
    grad_down = dot(dy_all, act[:, :hids], 0, 0).astype(bf)
    down_sums = lax.psum_scatter(grad_down, "dp", scatter_dimension=0, tiled=True)
    down_sums = lax.optimization_barrier(down_sums)
    d_pre = after(d_pre, grad_down)
    grad_up = dot(xn2, d_pre[:, :hids], 0, 0).astype(bf)
    if halving:
        up_sums, step = grad_up.reshape(ring, here, hids), 1
        pending = exchange_half(up_sums, "dp", step)
    else:
        up_sums, step, pending = lax.psum_scatter(grad_up, "dp", tiled=True), ring, ()

    def next_half(pending, step, *others):
        if not halving or step == ring:
            return pending, step
        keep, got = pending
        if others:
            got = after(got, *others)
        total = (keep.astype(fl) + got.astype(fl)).astype(bf)
        step *= 2
        if step == ring:
            return total, step
        return exchange_half(total, "dp", step), step

    d_h1, d_h1_b, d_qkv = [], [], ()
    g2, c2, bo = 0.0, 0.0, 0.0
    for i in range(images):
        at = slice(i * size, (i + 1) * size)
        got = after(received[i], grad_up, grad_down, *d_qkv)
        total = dxn_parts[i].astype(fl)
        for other in got:
            total = total + other.astype(fl)
        back, hat = normalize_back(h1[at], mean2[at], inverse2[at], ln_gain[1], total)
        g2 = g2 + jnp.sum(total * hat, axis=0)
        c2 = c2 + jnp.sum(total, axis=0)
        full = dy_all[at].astype(fl) + back
        bo = bo + jnp.sum(full, axis=0)
        d_h1.append(full)
        d_h1_b.append(full.astype(bf))
        d_att = dot(d_h1_b[i], own_out, 1, 0).astype(bf)
        d_qkv = (
            attention_backward(qkv, key_bias, attended[i], d_att, lses[i], d_qkv, i, size, heads),
        )
        if i < images - 1:
            pending, step = next_half(pending, step, *d_qkv)
    (d_qkv,) = d_qkv

    y_parts = after(y_parts, got)
    y_shares = send_blocks(y_parts, where, parts, rowp)

    grad_qkv = dot(xn1, d_qkv, 0, 0).astype(bf)
    grad_out = dot(jnp.concatenate(d_h1_b, axis=0), attended_all, 0, 0).astype(bf)
    att_grads = jnp.concatenate([grad_qkv, grad_out], axis=1)
    att_sums = lax.psum_scatter(att_grads, "dp", scatter_dimension=0, tiled=True)

    pending, step = next_half(pending, step, att_grads)
    d_qkv = after(d_qkv, att_grads, *pending[:1])
    sums_qkv = jnp.sum(d_qkv.astype(fl), axis=0)
    d_xn1 = dot(d_qkv, full_qkv, 1, 1).astype(bf).reshape(images, size, width)
    d_xn1 = [d_xn1[i] for i in range(images)]
    shares = send_blocks(d_xn1, where, parts, rowp)
    y_shares = after(y_shares, *d_xn1)
    h1_own = lax.dynamic_slice_in_dim(h1.reshape(images, size, width), where * rowp, rowp, 1)
    y_own = h1_own + sum_of(y_shares) + out_bias[1]
    output = jnp.where(own_valid, y_own, 0.0).astype(bf)
    pending, step = next_half(pending, step, *d_xn1)
    if halving:
        shares = after(shares, *pending[:1])
    d_xn1 = sum_of(shares)

    def own_part(values):
        return lax.dynamic_slice_in_dim(values.reshape(images, size, 1), where * rowp, rowp, 1)

    back, hat = normalize_back(
        x_own.astype(fl), own_part(mean1), own_part(inverse1), ln_gain[0], d_xn1
    )
    g1 = jnp.sum(d_xn1 * hat, axis=(0, 1))
    c1 = jnp.sum(d_xn1, axis=(0, 1))
    d_h1_own = jnp.stack([lax.dynamic_slice_in_dim(d, where * rowp, rowp, 0) for d in d_h1])
    d_inputs = (d_h1_own + back).astype(bf)

    b2 = jnp.sum(dy_own.astype(fl), axis=(0, 1))
    pair = jnp.stack([g1, g2 / parts, c1, c2 / parts, bo / parts, b2])
    pair = sum_everywhere(pair, "tensor")
    lone = jnp.concatenate([sums_qkv[:cols], sums_qkv[2 * colp : 2 * colp + cols], grad_b1[:hidden]])
    small = sum_everywhere(jnp.concatenate([pair.reshape(-1), lone]), "dp")
    pair = small[: 6 * width].reshape(6, width)
    lone = small[6 * width :]

    while halving and step < ring:
        pending, step = next_half(pending, step)
    if halving:
        up_sums = pending[0]

    def own_rows(values):
        return jnp.transpose(values[:, :rows], (1, 0, 2))

    return (
        own_rows(output),
        own_rows(d_inputs),
        pair[0:2],
        pair[2:4],
        att_sums[:, : 3 * colp].reshape(here, 3, colp)[:, :, :cols].astype(fl),
        lone[: 2 * cols].reshape(2, cols),
        transposed(att_sums[:, 3 * colp : 3 * colp + cols]),
        pair[4:6],
        up_sums[:, :hidden].astype(fl),
        lone[2 * cols :],
        transposed(down_sums)[:hidden],
    )


def solution(mesh):
    return jax.shard_map(
        on_device,
        mesh=mesh,
        in_specs=(
            P("tensor", "dp", None),
            P("dp"),
            P("tensor", "dp", None),
            P(),
            P(),
            P("dp", None, "tensor"),
            P(None, "tensor"),
            P("tensor", "dp"),
            P(),
            P("dp", "tensor"),
            P("tensor"),
            P("tensor", "dp"),
        ),
        out_specs=(
            P("tensor", "dp", None),
            P("tensor", "dp", None),
            P(),
            P(),
            P("dp", None, "tensor"),
            P(None, "tensor"),
            P("tensor", "dp"),
            P(),
            P("dp", "tensor"),
            P("tensor"),
            P("tensor", "dp"),
        ),
        check_vma=False,
    )
```
